32 devices in a mesh: band: 4 (over y, core), grid: 8 (over z, x).
Axes of the slice: x: 2, y: 2, z: 4, core: 2. Of those that a mesh axis runs over, the one named last changes fastest.
Arguments:
- wave: float32 [128, 64, 64, 128], P('grid', 'band'), may hold values from -1400 to 1400
- direction: float32 [128, 64, 64, 128], P('grid', 'band'), may hold values from -6 to 6
- potential: float32 [64, 64, 128], P('band', 'grid'), may hold values from -50 to 50
- rotation: float32 [384, 128], replicated, may hold values from -0.3125 to 0.3125
Outputs:
- new_block: float32 [128, 64, 64, 128], P(None, 'band', 'grid')
The draws below stay inside these ranges and needn't reach their ends.
All inputs are finite; a program needn't handle non-finite values.
Results may differ from the reference program's by a relative error of at most 0.00016.
Values sent between devices are 32-bit elements; how exact they have to be, the bound alone decides.
No kernel may reach another device: no remote copies, remote signals or barrier semaphores. Data moves between devices by JAX's collectives and lax.ppermute only.
A program may use at most 704 MiB of HBM per device.

```python
import math
import jax
import jax.numpy as jnp
from jax import lax

NB = 128
NX = 64
NY = 64
NZ = 128


def draw_wave(key, part):
    base = jax.random.fold_in(key, 31)
    keys = jax.random.split(base, 3)
    shape = (NB, NX, NY, NZ)
    noise = jax.random.truncated_normal(keys[0], -4.0, 4.0, shape, jnp.float32)
    slope_rate = math.log(3.0)
    cell_scale = jnp.exp(math.log(10.0) * jax.random.uniform(keys[1], (1, NX, NY, NZ), jnp.float32))
    band_scale = jnp.exp(math.log(10.0) * jax.random.uniform(keys[2], (NB, 1, 1, 1), jnp.float32))
    position = jnp.arange(NX, dtype=jnp.float32) / NX
    slope = jnp.exp(0.5 * slope_rate * position)[None, :, None, None]
    return noise * cell_scale * band_scale * slope


def draw_potential(key, part):
    base = jax.random.fold_in(key, 47)
    keys = jax.random.split(base, 2)
    phase = jax.random.uniform(keys[0], (), jnp.float32, 0.0, 2.0 * math.pi)
    along_x = 2.0 * math.pi * jnp.arange(NX, dtype=jnp.float32) / NX
    smooth = 24.0 * jnp.cos(along_x + phase)[:, None, None] + jnp.zeros((1, NY, 1), jnp.float32)
    noise = jax.random.uniform(keys[1], (NX, NY, NZ), jnp.float32, -10.0, 10.0)
    return smooth + noise


def steps_of(rng, extent, shards, least, top_value):
    gain = 1.0
    for dim, blocks in shards:
        draws = jax.random.uniform(jax.random.fold_in(jax.random.fold_in(rng, 6), dim), (blocks,), jnp.float32, least / len(shards), top_value / len(shards))
        gain = gain * jnp.repeat(jnp.exp(draws), extent[dim] // blocks).reshape((-1,) + (1,) * (len(extent) - 1 - dim))
    return gain


def centred(own_key, dims, spread, reach, shards=(), kind=jnp.bfloat16):
    drawn = jax.random.normal(own_key, dims, jnp.float32) * spread
    if len(shards) > 0:
        drawn = steps_of(own_key, dims, shards, -0.22, 0.18) * drawn
    return jnp.clip(drawn, min=-reach, max=reach).astype(kind)


def setup_inputs(seed: int = 0) -> dict:
    splits = jax.random.split(jax.random.key(seed), 5)
    return {
        "wave": draw_wave(jax.random.fold_in(splits[4], 71), 0),
        "direction": centred(splits[1], (NB, NX, NY, NZ), 1.0, 6.0, ((0, 8), (1, 4)), jnp.float32),
        "potential": draw_potential(jax.random.fold_in(splits[4], 71), 0),
        "rotation": centred(splits[3], (3 * NB, NB), (3 * NB) ** -0.5, 0.3125, (), jnp.float32),
    }


STENCIL = (-5369.0 / 1800.0, 12.0 / 7.0, -15.0 / 56.0, 10.0 / 189.0, -1.0 / 112.0, 2.0 / 1925.0, -1.0 / 16632.0)
LATTICE = 51.3

def axis_term(field, axis):
    total = STENCIL[0] * field
    for offset in range(1, 7):
        total = total + STENCIL[offset] * (jnp.roll(field, offset, axis) + jnp.roll(field, -offset, axis))
    return total

def reference(wave, direction, potential, rotation):
    bands, planes, rows_y, depth = wave.shape
    inverse_x = (planes / LATTICE) ** 2
    inverse_y = (rows_y / LATTICE) ** 2
    inverse_z = (depth / LATTICE) ** 2
    second = axis_term(wave, 1) * inverse_x + axis_term(wave, 2) * inverse_y + axis_term(wave, 3) * inverse_z
    hwave = -0.5 * second + potential[None] * wave
    numer = jnp.sum(wave * hwave, axis=(1, 2, 3))
    denom = jnp.sum(wave * wave, axis=(1, 2, 3))
    ritz = numer / denom
    resid = hwave - ritz[:, None, None, None] * wave
    ncells = planes * rows_y * depth
    groups = [resid.reshape(bands, ncells), wave.reshape(bands, ncells), direction.reshape(bands, ncells)]
    high = lax.Precision.HIGHEST
    rows_list = []
    for first in range(3):
        row_blocks = []
        for second_index in range(3):
            row_blocks.append(jnp.dot(groups[first], groups[second_index].T, precision=high) / ncells)
        rows_list.append(jnp.concatenate(row_blocks, axis=1))
    gram = jnp.concatenate(rows_list, axis=0)
    factor = jnp.linalg.cholesky(gram)
    solved = jax.scipy.linalg.solve_triangular(factor, rotation, lower=True, trans=1)
    result = jnp.zeros((bands, ncells), jnp.float32)
    for first in range(3):
        result = result + jnp.dot(solved[first * bands:(first + 1) * bands].T, groups[first], precision=high)
    return result.reshape(bands, planes, rows_y, depth)
```

```python
import functools

import jax
import jax.numpy as jnp
from jax import lax
from jax.experimental import pallas as pl
from jax.experimental.pallas import tpu as pltpu
from jax.sharding import PartitionSpec as P

STENCIL = (
    -5369.0 / 1800.0,
    12.0 / 7.0,
    -15.0 / 56.0,
    10.0 / 189.0,
    -1.0 / 112.0,
    2.0 / 1925.0,
    -1.0 / 16632.0,
)
LATTICE = 51.3
WIDTH = len(STENCIL) - 1
HIGH = lax.Precision.HIGHEST
F32 = jnp.float32
BF16 = jnp.bfloat16


def halos(shard, axis, dim):
    devices, length = lax.axis_size(axis), shard.shape[dim]
    up = [(i, (i + 1) % devices) for i in range(devices)]
    down = [(j, i) for i, j in up]
    last = lax.slice_in_dim(shard, length - WIDTH, length, axis=dim)
    first = lax.slice_in_dim(shard, 0, WIDTH, axis=dim)
    return lax.ppermute(last, axis, up), lax.ppermute(first, axis, down)


def butterfly_sum(value):
    for axis in ("band", "grid"):
        devices, step = lax.axis_size(axis), 1
        while step < devices:
            value = value + lax.ppermute(
                value, axis, [(i, i ^ step) for i in range(devices)]
            )
            step *= 2
    return value


def kinetic_kernel(weights, w_ref, lo_ref, hi_ref, t_ref, s_ref, pad):
    _, planes, rows, depth = w_ref.shape
    parts, _, _, mine, _ = t_ref.shape
    center, along_x, along_y, along_z = weights
    pad[0:WIDTH] = lo_ref[0]
    pad[WIDTH : WIDTH + planes] = w_ref[0]
    pad[WIDTH + planes :] = hi_ref[0]

    def plane(i, total):
        here = pad[i + WIDTH]
        out = center * here
        for k in range(1, WIDTH + 1):
            out += along_x[k - 1] * (pad[i + WIDTH + k] + pad[i + WIDTH - k])
            out += along_y[k - 1] * (
                pltpu.roll(here, k, 0) + pltpu.roll(here, rows - k, 0)
            )
            out += along_z[k - 1] * (
                pltpu.roll(here, k, 1) + pltpu.roll(here, depth - k, 1)
            )
        t_ref[:, 0, i] = out.reshape(parts, mine, depth)
        return total + (here * out).reshape(-1, 8, depth).sum(0)

    s_ref[0] = lax.fori_loop(0, planes, plane, jnp.zeros((8, depth), F32))


def kinetic(wave, before, after, weights, parts):
    bands, planes, rows, depth = wave.shape
    spec = lambda n: pl.BlockSpec((1, n, rows, depth), lambda b: (b, 0, 0, 0))
    return pl.pallas_call(
        functools.partial(kinetic_kernel, weights),
        grid=(bands,),
        in_specs=[spec(planes), spec(WIDTH), spec(WIDTH)],
        out_specs=[
            pl.BlockSpec(
                (parts, 1, planes, rows // parts, depth), lambda b: (0, b, 0, 0, 0)
            ),
            pl.BlockSpec((1, 8, depth), lambda b: (b, 0, 0)),
        ],
        out_shape=[
            jax.ShapeDtypeStruct((parts, bands, planes, rows // parts, depth), F32),
            jax.ShapeDtypeStruct((bands, 8, depth), F32),
        ],
        scratch_shapes=[pltpu.VMEM((planes + 2 * WIDTH, rows, depth), F32)],
        compiler_params=pltpu.CompilerParams(vmem_limit_bytes=32 << 20),
        cost_estimate=pl.CostEstimate(
            flops=60 * wave.size, bytes_accessed=11 * wave.size, transcendentals=0
        ),
        name="kinetic",
    )(wave, before, after)


def split(value):
    high = value.astype(BF16)
    return high, (value - high.astype(F32)).astype(BF16)


def dot_t(a, b, precision=None):
    return lax.dot_general(
        a, b, (((1,), (1,)), ((), ())), precision=precision, preferred_element_type=F32
    )


def dot(a, b, precision=None):
    return jnp.dot(a, b, precision=precision, preferred_element_type=F32)


def row_of(ref, i):
    bands, planes, mine, depth = ref.shape
    flat = ref.reshape(bands * planes * mine, depth)
    return flat[pl.ds(i, bands, stride=planes * mine), :]


def split_rows(ref):
    count = ref.shape[1] * ref.shape[2]
    highs, lows = zip(*(split(row_of(ref, i)) for i in range(count)))
    return jnp.concatenate(highs, axis=1), jnp.concatenate(lows, axis=1)


def gram_pair_kernel(t_ref, w_ref, v_ref, ritz_ref, g_ref, high_ref, low_ref, acc, cross):
    step, last = pl.program_id(0), pl.num_programs(0) - 1
    _, planes, mine, depth = w_ref.shape

    @pl.when(step == 0)
    def _():
        acc[...] = jnp.zeros_like(acc)
        cross[...] = jnp.zeros_like(cross)

    for i in range(planes * mine):
        w = row_of(w_ref, i)
        x, y = i // mine, i % mine
        r = row_of(t_ref, i) + (v_ref[x, y : y + 1, :] - ritz_ref[...]) * w
        high, low = split(jnp.concatenate([r, w], axis=0))
        high_ref[:, i * depth : (i + 1) * depth] = high
        low_ref[:, i * depth : (i + 1) * depth] = low
    high = high_ref[...]
    acc[...] += dot_t(high, high)
    cross[...] += dot_t(high, low_ref[...])

    @pl.when(step == last)
    def _():
        g_ref[...] = acc[...] + (cross[...] + cross[...].T)


def gram_row_kernel(high_ref, low_ref, d_ref, g_ref, acc):
    step, last = pl.program_id(0), pl.num_programs(0) - 1
    bands = d_ref.shape[0]

    @pl.when(step == 0)
    def _():
        acc[...] = jnp.zeros_like(acc)

    high, low = split_rows(d_ref)
    both = jnp.concatenate([high, low], axis=0)
    wide = dot_t(jnp.concatenate([high_ref[...], high], axis=0), both)
    acc[...] += wide[:, :bands] + wide[:, bands:]
    rest = dot_t(jnp.concatenate([low_ref[...], low], axis=0), high)
    acc[...] += rest

    @pl.when(step == last)
    def _():
        g_ref[...] = acc[...].T


def apply_kernel(high_ref, low_ref, d_ref, c_ref, o_ref):
    bands, planes, mine, depth = o_ref.shape
    d_high, d_low = split_rows(d_ref)
    c_high, c_low = split(c_ref[...])
    wide = dot(
        jnp.concatenate([c_high, c_low], axis=0),
        jnp.concatenate([high_ref[...], d_high], axis=0),
    )
    out = wide[:bands] + wide[bands:]
    out += dot(c_high, jnp.concatenate([low_ref[...], d_low], axis=0))
    flat = o_ref.reshape(bands * planes * mine, depth)
    for i in range(planes * mine):
        flat[pl.ds(i, bands, stride=planes * mine), :] = out[:, i * depth : (i + 1) * depth]


def tile_spec(bands, planes, mine, depth):
    return pl.BlockSpec((bands, planes, mine, depth), lambda x: (0, x, 0, 0))


def cost(flops, nbytes):
    return pl.CostEstimate(flops=flops, bytes_accessed=nbytes, transcendentals=0)


STEP = 2


def gram_pair(t, w, v, ritz):
    bands, planes, mine, depth = w.shape
    tile = tile_spec(bands, STEP, mine, depth)
    points = pl.BlockSpec((2 * bands, STEP * mine * depth), lambda x: (0, x))
    parts = jax.ShapeDtypeStruct((2 * bands, planes * mine * depth), BF16)
    square = (2 * bands, 2 * bands)
    return pl.pallas_call(
        gram_pair_kernel,
        grid=(planes // STEP,),
        in_specs=[
            tile,
            tile,
            pl.BlockSpec((STEP, mine, depth), lambda x: (x, 0, 0)),
            pl.BlockSpec((bands, depth), lambda x: (0, 0)),
        ],
        out_specs=[pl.BlockSpec(square, lambda x: (0, 0)), points, points],
        out_shape=[jax.ShapeDtypeStruct(square, F32), parts, parts],
        scratch_shapes=[pltpu.VMEM(square, F32), pltpu.VMEM(square, F32)],
        compiler_params=pltpu.CompilerParams(vmem_limit_bytes=40 << 20),
        cost_estimate=cost(16 * bands * w.size, 16 * w.size),
        name="gram_pair",
    )(t, w, v, ritz)


def gram_row(high, low, d):
    bands, planes, mine, depth = d.shape
    points = pl.BlockSpec((2 * bands, STEP * mine * depth), lambda x: (0, x))
    return pl.pallas_call(
        gram_row_kernel,
        grid=(planes // STEP,),
        in_specs=[points, points, tile_spec(bands, STEP, mine, depth)],
        out_specs=pl.BlockSpec((bands, 3 * bands), lambda x: (0, 0)),
        out_shape=jax.ShapeDtypeStruct((bands, 3 * bands), F32),
        scratch_shapes=[pltpu.VMEM((3 * bands, bands), F32)],
        compiler_params=pltpu.CompilerParams(vmem_limit_bytes=40 << 20),
        cost_estimate=cost(18 * bands * d.size, 12 * d.size),
        name="gram_row",
    )(high, low, d)


def apply_basis(high, low, d, coefficients):
    bands, planes, mine, depth = d.shape
    points = pl.BlockSpec((2 * bands, STEP * mine * depth), lambda x: (0, x))
    tile = tile_spec(bands, STEP, mine, depth)
    return pl.pallas_call(
        apply_kernel,
        grid=(planes // STEP,),
        in_specs=[points, points, tile, pl.BlockSpec((bands, 3 * bands), lambda x: (0, 0))],
        out_specs=tile,
        out_shape=jax.ShapeDtypeStruct(d.shape, F32),
        compiler_params=pltpu.CompilerParams(vmem_limit_bytes=40 << 20),
        cost_estimate=cost(18 * bands * d.size, 16 * d.size),
        name="apply_basis",
    )(high, low, d, coefficients)


def spread_row(value, i):
    return jnp.broadcast_to(value[i : i + 1, :], value.shape)


def spread_column(value, j):
    return jnp.broadcast_to(value[:, j : j + 1], value.shape)


def inverse_factor(matrix):
    size = matrix.shape[0]
    count = size // 8
    shape = (8, size)
    sublane = lax.broadcasted_iota(jnp.int32, shape, 0)
    lane = lax.broadcasted_iota(jnp.int32, shape, 1)
    left = [matrix[8 * q : 8 * q + 8] for q in range(count)]
    right = [jnp.where(lane == sublane + 8 * q, 1.0, 0.0).astype(F32) for q in range(count)]
    done = []
    for p in range(count):
        base = 8 * p
        rows = [spread_row(left[p], i) for i in range(8)]
        ones = [spread_row(right[p], i) for i in range(8)]
        entry = {
            (i, j): spread_column(rows[i], base + j) for i in range(8) for j in range(i, 8)
        }
        unit, inverse = {}, []
        for k in range(8):
            inverse.append(1.0 / entry[k, k])
            for i in range(k + 1, 8):
                unit[i, k] = entry[k, i] * inverse[k]
            for i in range(k + 1, 8):
                for j in range(i, 8):
                    entry[i, j] = entry[i, j] - unit[i, k] * entry[k, j]
        for i in range(8):
            for k in range(i):
                rows[i] = rows[i] - unit[i, k] * rows[k]
                ones[i] = ones[i] - unit[i, k] * ones[k]
        out = ones[0] * lax.rsqrt(entry[0, 0])
        for i in range(1, 8):
            out = jnp.where(sublane == i, ones[i] * lax.rsqrt(entry[i, i]), out)
        done.append(out)
        if p == count - 1:
            break
        for i in reversed(range(8)):
            rows[i] = rows[i] * inverse[i]
            ones[i] = ones[i] * inverse[i]
            for k in range(i + 1, 8):
                rows[i] = rows[i] - unit[k, i] * rows[k]
                ones[i] = ones[i] - unit[k, i] * ones[k]
        for q in range(p + 1, count):
            columns = [spread_column(left[q], base + i) for i in range(8)]
            for i in range(8):
                left[q] = left[q] - columns[i] * rows[i]
                right[q] = right[q] - columns[i] * ones[i]
    return jnp.concatenate(done, axis=0)


def factor_pair_kernel(scale, g_ref, o_ref):
    half = g_ref.shape[0] // 2
    first = inverse_factor(g_ref[:half, :half] * scale)
    lower = dot_t(g_ref[half:, :half] * scale, first, HIGH)
    second = inverse_factor(g_ref[half:, half:] * scale - dot_t(lower, lower, HIGH))
    o_ref[:half, :half] = first
    o_ref[:half, half:] = jnp.zeros((half, half), F32)
    o_ref[half:, :half] = -dot(second, dot(lower, first, HIGH), HIGH)
    o_ref[half:, half:] = second


def factor_pair(gram, scale):
    return pl.pallas_call(
        functools.partial(factor_pair_kernel, scale),
        out_shape=jax.ShapeDtypeStruct(gram.shape, F32),
        cost_estimate=cost(10**8, 4 * gram.size),
        name="factor_pair",
    )(gram)


def coefficients_kernel(scale, row_ref, pair_ref, turned_ref, o_ref):
    bands = row_ref.shape[0]
    pair = pair_ref[...]
    lower = dot_t(row_ref[:, : 2 * bands] * scale, pair, HIGH)
    last = inverse_factor(row_ref[:, 2 * bands :] * scale - dot_t(lower, lower, HIGH))
    tail = dot(turned_ref[:, 2 * bands :], last, HIGH)
    o_ref[:, 2 * bands :] = tail
    o_ref[:, : 2 * bands] = dot(turned_ref[:, : 2 * bands] - dot(tail, lower, HIGH), pair, HIGH)


def coefficients_of(row, pair, turned, scale):
    return pl.pallas_call(
        functools.partial(coefficients_kernel, scale),
        out_shape=jax.ShapeDtypeStruct(row.shape, F32),
        cost_estimate=cost(10**8, 4 * row.size),
        name="coefficients",
    )(row, pair, turned)


def fast(wave, direction, potential, rotation):
    bands_here, planes, rows_y, depth = wave.shape
    parts = lax.axis_size("grid")
    bands, mine = bands_here * parts, rows_y // parts
    total_x = planes * lax.axis_size("band")
    scale = [-0.5 * (n / LATTICE) ** 2 for n in (total_x, rows_y, depth)]
    weights = (
        STENCIL[0] * sum(scale),
        *([s * c for c in STENCIL[1:]] for s in scale),
    )
    ncells = total_x * rows_y * depth

    def pack(field):
        cut = field.reshape(bands_here, planes, parts, mine, depth)
        return cut.transpose(2, 0, 1, 3, 4)

    def exchange(blocks):
        got = lax.all_to_all(blocks, "grid", 0, 0, tiled=True)
        return got.reshape(bands, planes, mine, depth)

    before, after = halos(wave, "band", 1)
    w = exchange(pack(wave))
    sent, own = kinetic(wave, before, after, weights, parts)
    own = lax.dynamic_update_slice(
        jnp.zeros((bands,), F32),
        own.sum((1, 2)),
        (lax.axis_index("grid") * bands_here,),
    )
    square = w * w
    numer = own + jnp.sum(square * potential[None], axis=(1, 2, 3))
    sums = butterfly_sum(jnp.stack([numer, jnp.sum(square, axis=(1, 2, 3))]))
    t = exchange(sent)
    d_sent, sums = lax.optimization_barrier((pack(direction), sums))
    ritz = jnp.broadcast_to((sums[0] / sums[1])[:, None], (bands, depth))
    d = exchange(d_sent)

    pair, high, low = gram_pair(t, w, potential, ritz)
    pair = butterfly_sum(pair)
    row = gram_row(high, low, d)
    inverse = factor_pair(pair, 1.0 / ncells)
    row = butterfly_sum(row)
    solved = coefficients_of(row, inverse, rotation.T, 1.0 / ncells)
    return apply_basis(high, low, d, solved)


def axis_term(field, axis):
    total = STENCIL[0] * field
    for k in range(1, WIDTH + 1):
        total = total + STENCIL[k] * (jnp.roll(field, k, axis) + jnp.roll(field, -k, axis))
    return total


def general(wave, direction, potential, rotation):
    bands_here, planes, rows_y, depth = wave.shape
    total_x = planes * lax.axis_size("band")
    inverse_x, inverse_y, inverse_z = ((n / LATTICE) ** 2 for n in (total_x, rows_y, depth))
    before, after = halos(wave, "band", 1)
    padded = jnp.concatenate([before, wave, after], axis=1)
    along_x = STENCIL[0] * wave
    for k in range(1, WIDTH + 1):
        along_x = along_x + STENCIL[k] * (
            padded[:, WIDTH + k : WIDTH + k + planes]
            + padded[:, WIDTH - k : WIDTH - k + planes]
        )
    second = along_x * inverse_x + axis_term(wave, 2) * inverse_y + axis_term(wave, 3) * inverse_z
    local_pot = lax.all_gather(potential, "grid", axis=1, tiled=True)
    hwave = -0.5 * second + local_pot[None] * wave
    numer = jnp.sum(wave * hwave, axis=(1, 2, 3))
    denom = jnp.sum(wave * wave, axis=(1, 2, 3))
    numer, denom = lax.psum((numer, denom), "band")
    resid = hwave - (numer / denom)[:, None, None, None] * wave
    gathered = [
        lax.all_to_all(f, "grid", split_axis=2, concat_axis=0, tiled=True)
        for f in (resid, wave, direction)
    ]
    out_shape = gathered[0].shape
    stacked = jnp.concatenate(gathered, axis=0).reshape(3 * out_shape[0], -1)
    ncells = total_x * rows_y * depth
    gram = lax.psum(jnp.dot(stacked, stacked.T, precision=HIGH) / ncells, ("band", "grid"))
    factor = jnp.linalg.cholesky(gram)
    solved = jax.scipy.linalg.solve_triangular(factor, rotation, lower=True, trans=1)
    mixed = lax.dot_general(solved, stacked, (((0,), (0,)), ((), ())), precision=HIGH)
    return mixed.reshape(out_shape)


def on_device(wave, direction, potential, rotation):
    _, planes, rows_y, depth = wave.shape
    mine = rows_y // lax.axis_size("grid")
    tiled = mine == 8 and depth == 128 and planes % STEP == 0
    return (fast if tiled else general)(wave, direction, potential, rotation)


def solution(mesh):
    return jax.shard_map(
        on_device,
        mesh=mesh,
        in_specs=(
            P("grid", "band", None, None),
            P("grid", "band", None, None),
            P("band", "grid", None),
            P(),
        ),
        out_specs=P(None, "band", "grid", None),
        check_vma=False,
    )
```

```python
import functools

import jax
import jax.numpy as jnp
from jax import lax
from jax.experimental import pallas as pl
from jax.experimental.pallas import tpu as pltpu
from jax.sharding import PartitionSpec as P

STENCIL = (
    -5369.0 / 1800.0,
    12.0 / 7.0,
    -15.0 / 56.0,
    10.0 / 189.0,
    -1.0 / 112.0,
    2.0 / 1925.0,
    -1.0 / 16632.0,
)
LATTICE = 51.3
WIDTH = len(STENCIL) - 1
HIGH = lax.Precision.HIGHEST
F32 = jnp.float32
BF16 = jnp.bfloat16


def halos(shard, axis, dim):
    devices, length = lax.axis_size(axis), shard.shape[dim]
    up = [(i, (i + 1) % devices) for i in range(devices)]
    down = [(j, i) for i, j in up]
    last = lax.slice_in_dim(shard, length - WIDTH, length, axis=dim)
    first = lax.slice_in_dim(shard, 0, WIDTH, axis=dim)
    return lax.ppermute(last, axis, up), lax.ppermute(first, axis, down)


def butterfly_sum(value):
    for axis in ("band", "grid"):
        devices, step = lax.axis_size(axis), 1
        while step < devices:
            value = value + lax.ppermute(
                value, axis, [(i, i ^ step) for i in range(devices)]
            )
            step *= 2
    return value


def halved_sum(value):
    half = value.shape[0] // 2
    bands, odd = lax.axis_size("band"), lax.axis_index("band") % 2 == 1
    swap = [(i, i ^ 1) for i in range(bands)]
    top, bottom = value[:half], value[half:]
    mine = jnp.where(odd, bottom, top)
    mine = mine + lax.ppermute(jnp.where(odd, top, bottom), "band", swap)
    for axis, step in (("band", 2), ("grid", 1)):
        devices = lax.axis_size(axis)
        while step < devices:
            mine = mine + lax.ppermute(
                mine, axis, [(i, i ^ step) for i in range(devices)]
            )
            step *= 2
    other = lax.ppermute(mine, "band", swap)
    return jnp.concatenate([jnp.where(odd, other, mine), jnp.where(odd, mine, other)])


def kinetic_kernel(weights, w_ref, lo_ref, hi_ref, t_ref, s_ref, pad):
    _, planes, rows, depth = w_ref.shape
    parts, _, _, mine, _ = t_ref.shape
    center, along_x, along_y, along_z = weights
    pad[0:WIDTH] = lo_ref[0]
    pad[WIDTH : WIDTH + planes] = w_ref[0]
    pad[WIDTH + planes :] = hi_ref[0]

    def plane(i, total):
        here = pad[i + WIDTH]
        out = center * here
        for k in range(1, WIDTH + 1):
            out += along_x[k - 1] * (pad[i + WIDTH + k] + pad[i + WIDTH - k])
            out += along_y[k - 1] * (
                pltpu.roll(here, k, 0) + pltpu.roll(here, rows - k, 0)
            )
            out += along_z[k - 1] * (
                pltpu.roll(here, k, 1) + pltpu.roll(here, depth - k, 1)
            )
        t_ref[:, 0, i] = out.reshape(parts, mine, depth)
        return total + (here * out).reshape(-1, 8, depth).sum(0)

    s_ref[0] = lax.fori_loop(0, planes, plane, jnp.zeros((8, depth), F32))


def kinetic(wave, before, after, weights, parts):
    bands, planes, rows, depth = wave.shape
    spec = lambda n: pl.BlockSpec((1, n, rows, depth), lambda b: (b, 0, 0, 0))
    return pl.pallas_call(
        functools.partial(kinetic_kernel, weights),
        grid=(bands,),
        in_specs=[spec(planes), spec(WIDTH), spec(WIDTH)],
        out_specs=[
            pl.BlockSpec(
                (parts, 1, planes, rows // parts, depth), lambda b: (0, b, 0, 0, 0)
            ),
            pl.BlockSpec((1, 8, depth), lambda b: (b, 0, 0)),
        ],
        out_shape=[
            jax.ShapeDtypeStruct((parts, bands, planes, rows // parts, depth), F32),
            jax.ShapeDtypeStruct((bands, 8, depth), F32),
        ],
        scratch_shapes=[pltpu.VMEM((planes + 2 * WIDTH, rows, depth), F32)],
        compiler_params=pltpu.CompilerParams(vmem_limit_bytes=32 << 20),
        cost_estimate=pl.CostEstimate(
            flops=60 * wave.size, bytes_accessed=11 * wave.size, transcendentals=0
        ),
        name="kinetic",
    )(wave, before, after)


def split(value):
    high = value.astype(BF16)
    return high, (value - high.astype(F32)).astype(BF16)


def dot_t(a, b, precision=None):
    return lax.dot_general(
        a, b, (((1,), (1,)), ((), ())), precision=precision, preferred_element_type=F32
    )


def dot(a, b, precision=None):
    return jnp.dot(a, b, precision=precision, preferred_element_type=F32)


def row_of(ref, i):
    bands, planes, mine, depth = ref.shape
    flat = ref.reshape(bands * planes * mine, depth)
    return flat[pl.ds(i, bands, stride=planes * mine), :]


def split_rows(ref):
    count = ref.shape[1] * ref.shape[2]
    highs, lows = zip(*(split(row_of(ref, i)) for i in range(count)))
    return jnp.concatenate(highs, axis=1), jnp.concatenate(lows, axis=1)


def gram_pair_kernel(t_ref, w_ref, v_ref, ritz_ref, g_ref, parts_ref, acc, cross):
    step, last = pl.program_id(0), pl.num_programs(0) - 1
    bands, planes, mine, depth = w_ref.shape

    @pl.when(step == 0)
    def _():
        acc[...] = jnp.zeros_like(acc)
        cross[...] = jnp.zeros_like(cross)

    for i in range(planes * mine):
        w = row_of(w_ref, i)
        x, y = i // mine, i % mine
        r = row_of(t_ref, i) + (v_ref[x, y : y + 1, :] - ritz_ref[...]) * w
        high, low = split(jnp.concatenate([r, w], axis=0))
        parts_ref[: 2 * bands, i * depth : (i + 1) * depth] = high
        parts_ref[2 * bands :, i * depth : (i + 1) * depth] = low
    high = parts_ref[: 2 * bands]
    acc[...] += dot_t(high, high)
    cross[...] += dot_t(high, parts_ref[2 * bands :])

    @pl.when(step == last)
    def _():
        g_ref[...] = acc[...] + (cross[...] + cross[...].T)


def gram_row_kernel(parts_ref, d_ref, so_far_ref, g_ref, both_ref):
    points = parts_ref.shape[0]

    @pl.when(pl.program_id(0) == 0)
    def _():
        g_ref[...] = so_far_ref[...]

    both = jnp.concatenate(split_rows(d_ref), axis=0)
    both_ref[...] = both
    g_ref[:, :points] += dot_t(both, parts_ref[...])
    g_ref[:, points:] += dot_t(both, both)


def apply_points(parts, both, c_ref, o_ref):
    bands, planes, mine, depth = o_ref.shape
    high, low = split(c_ref[...])
    pair, last = slice(0, 2 * bands), slice(2 * bands, 3 * bands)
    stacked = jnp.concatenate([high[:, pair], low[:, pair]], axis=0)
    ending = jnp.concatenate(
        [
            jnp.concatenate([high[:, last], high[:, last]], axis=1),
            jnp.concatenate([low[:, last], jnp.zeros_like(low[:, last])], axis=1),
        ],
        axis=0,
    )
    wide = dot(stacked, parts[: 2 * bands]) + dot(ending, both)
    out = wide[:bands] + wide[bands:] + dot(high[:, pair], parts[2 * bands :])
    flat = o_ref.reshape(bands * planes * mine, depth)
    for i in range(planes * mine):
        flat[pl.ds(i, bands, stride=planes * mine), :] = out[:, i * depth : (i + 1) * depth]


def tile_spec(bands, planes, mine, depth):
    return pl.BlockSpec((bands, planes, mine, depth), lambda x: (0, x, 0, 0))


def cost(flops, nbytes):
    return pl.CostEstimate(flops=flops, bytes_accessed=nbytes, transcendentals=0)


STEP = 2
EARLY = 12


def gram_pair(t, w, v, ritz):
    bands, planes, mine, depth = w.shape
    tile = tile_spec(bands, STEP, mine, depth)
    points = pl.BlockSpec((4 * bands, STEP * mine * depth), lambda x: (0, x))
    parts = jax.ShapeDtypeStruct((4 * bands, planes * mine * depth), BF16)
    square = (2 * bands, 2 * bands)
    return pl.pallas_call(
        gram_pair_kernel,
        grid=(planes // STEP,),
        in_specs=[
            tile,
            tile,
            pl.BlockSpec((STEP, mine, depth), lambda x: (x, 0, 0)),
            pl.BlockSpec((bands, depth), lambda x: (0, 0)),
        ],
        out_specs=[pl.BlockSpec(square, lambda x: (0, 0)), points],
        out_shape=[jax.ShapeDtypeStruct(square, F32), parts],
        scratch_shapes=[pltpu.VMEM(square, F32), pltpu.VMEM(square, F32)],
        compiler_params=pltpu.CompilerParams(vmem_limit_bytes=60 << 20),
        cost_estimate=cost(16 * bands * w.size, 16 * w.size),
        name="gram_pair",
    )(t, w, v, ritz)


def gram_row(parts, d, so_far, skip):
    bands, planes, mine, depth = d.shape
    count = STEP * mine * depth
    whole = pl.BlockSpec(so_far.shape, lambda x: (0, 0))
    return pl.pallas_call(
        gram_row_kernel,
        grid=(planes // STEP,),
        in_specs=[
            pl.BlockSpec((4 * bands, count), lambda x: (0, x + skip // STEP)),
            tile_spec(bands, STEP, mine, depth),
            whole,
        ],
        out_specs=[whole, pl.BlockSpec((2 * bands, count), lambda x: (0, x))],
        out_shape=[
            jax.ShapeDtypeStruct(so_far.shape, F32),
            jax.ShapeDtypeStruct((2 * bands, planes * mine * depth), BF16),
        ],
        compiler_params=pltpu.CompilerParams(vmem_limit_bytes=(60 if skip == 0 else 40) << 20),
        cost_estimate=cost(18 * bands * d.size, 12 * d.size),
        name="gram_row",
    )(parts, d, so_far)


def joined(products):
    bands = products.shape[0] // 2
    wide = products[:bands] + products[bands:]
    pair = wide[:, : 2 * bands] + wide[:, 2 * bands : 4 * bands]
    own = wide[:, 4 * bands : 5 * bands] + wide[:, 5 * bands :]
    return jnp.concatenate([pair, own], axis=1)


def spread_row(value, i):
    return jnp.broadcast_to(value[i : i + 1, :], value.shape)


def spread_column(value, j):
    return jnp.broadcast_to(value[:, j : j + 1], value.shape)


def inverse_factor(matrix):
    size = matrix.shape[0]
    count = size // 8
    shape = (8, size)
    sublane = lax.broadcasted_iota(jnp.int32, shape, 0)
    lane = lax.broadcasted_iota(jnp.int32, shape, 1)
    left = [matrix[8 * q : 8 * q + 8] for q in range(count)]
    right = [jnp.where(lane == sublane + 8 * q, 1.0, 0.0).astype(F32) for q in range(count)]
    done = []
    for p in range(count):
        base = 8 * p
        rows = [spread_row(left[p], i) for i in range(8)]
        ones = [spread_row(right[p], i) for i in range(8)]
        entry = {
            (i, j): spread_column(rows[i], base + j) for i in range(8) for j in range(i, 8)
        }
        unit, inverse = {}, []
        for k in range(8):
            inverse.append(1.0 / entry[k, k])
            for i in range(k + 1, 8):
                unit[i, k] = entry[k, i] * inverse[k]
            for i in range(k + 1, 8):
                for j in range(i, 8):
                    entry[i, j] = entry[i, j] - unit[i, k] * entry[k, j]
        for i in range(8):
            for k in range(i):
                rows[i] = rows[i] - unit[i, k] * rows[k]
                ones[i] = ones[i] - unit[i, k] * ones[k]
        out = ones[0] * lax.rsqrt(entry[0, 0])
        for i in range(1, 8):
            out = jnp.where(sublane == i, ones[i] * lax.rsqrt(entry[i, i]), out)
        done.append(out)
        if p == count - 1:
            break
        for i in reversed(range(8)):
            rows[i] = rows[i] * inverse[i]
            ones[i] = ones[i] * inverse[i]
            for k in range(i + 1, 8):
                rows[i] = rows[i] - unit[k, i] * rows[k]
                ones[i] = ones[i] - unit[k, i] * ones[k]
        for q in range(p + 1, count):
            columns = [spread_column(left[q], base + i) for i in range(8)]
            for i in range(8):
                left[q] = left[q] - columns[i] * rows[i]
                right[q] = right[q] - columns[i] * ones[i]
    return jnp.concatenate(done, axis=0)


def factor_first_kernel(scale, g_ref, o_ref):
    o_ref[...] = inverse_factor(g_ref[...] * scale)


def factor_second_kernel(scale, g_ref, first_ref, o_ref):
    half = first_ref.shape[0]
    first = first_ref[...]
    lower = dot_t(g_ref[:, :half] * scale, first, HIGH)
    second = inverse_factor(g_ref[:, half:] * scale - dot_t(lower, lower, HIGH))
    o_ref[:half, :half] = first
    o_ref[:half, half:] = jnp.zeros((half, half), F32)
    o_ref[half:, :half] = -dot(second, dot(lower, first, HIGH), HIGH)
    o_ref[half:, half:] = second


def factor_pair(gram, scale):
    half = gram.shape[0] // 2
    first = pl.pallas_call(
        functools.partial(factor_first_kernel, scale),
        grid=(1,),
        in_specs=[pl.BlockSpec((half, half), lambda i: (0, 0))],
        out_specs=pl.BlockSpec((half, half), lambda i: (0, 0)),
        out_shape=jax.ShapeDtypeStruct((half, half), F32),
        cost_estimate=cost(10**9, gram.size),
        name="factor_first",
    )(gram)
    return pl.pallas_call(
        functools.partial(factor_second_kernel, scale),
        grid=(1,),
        in_specs=[
            pl.BlockSpec((half, 2 * half), lambda i: (1, 0)),
            pl.BlockSpec((half, half), lambda i: (0, 0)),
        ],
        out_specs=pl.BlockSpec((2 * half, 2 * half), lambda i: (0, 0)),
        out_shape=jax.ShapeDtypeStruct(gram.shape, F32),
        cost_estimate=cost(10**9, 4 * gram.size),
        name="factor_second",
    )(gram, first)


def finish_kernel(scale, row_ref, pair_ref, turned_ref, parts_hbm, early_hbm, late_hbm, o_ref, *scratch):
    parts_ref, both_ref, c_ref, sems = scratch
    step, bands = pl.program_id(0), row_ref.shape[0]
    count = parts_ref.shape[1] // pl.num_programs(0)
    cut = early_hbm.shape[1] // count

    @pl.when(step == 0)
    def _():
        for i in range(parts_ref.shape[1] // count):
            to = pl.ds(i * count, count)
            d_hbm, at = (early_hbm, i) if i < cut else (late_hbm, i - cut)
            own = d_hbm.at[:, pl.ds(at * count, count)]
            pltpu.make_async_copy(parts_hbm.at[:, to], parts_ref.at[:, to], sems.at[0, i]).start()
            pltpu.make_async_copy(own, both_ref.at[:, to], sems.at[1, i]).start()
        pair = pair_ref[...]
        lower = dot_t(row_ref[:, : 2 * bands] * scale, pair, HIGH)
        last = inverse_factor(row_ref[:, 2 * bands :] * scale - dot_t(lower, lower, HIGH))
        tail = dot(turned_ref[:, 2 * bands :], last, HIGH)
        c_ref[:, 2 * bands :] = tail
        rest = turned_ref[:, : 2 * bands] - dot(tail, lower, HIGH)
        c_ref[:, : 2 * bands] = dot(rest, pair, HIGH)

    here = pl.ds(pl.multiple_of(step * count, count), count)
    for to_ref, sem in ((parts_ref, sems.at[0, step]), (both_ref, sems.at[1, step])):
        pltpu.make_async_copy(to_ref.at[:, here], to_ref.at[:, here], sem).wait()
    apply_points(parts_ref[:, here], both_ref[:, here], c_ref, o_ref)


def finish(row, pair, turned, parts, early, late, scale, mine, depth):
    bands, points = row.shape[0], parts.shape[1]
    planes = points // (mine * depth)
    far = pl.BlockSpec(memory_space=pl.ANY)
    whole = lambda a: pl.BlockSpec(a.shape, lambda x: (0, 0), pipeline_mode=pl.Buffered(1))
    return pl.pallas_call(
        functools.partial(finish_kernel, scale),
        grid=(planes // STEP,),
        in_specs=[whole(row), whole(pair), whole(turned), far, far, far],
        out_specs=pl.BlockSpec((bands, STEP, mine, depth), lambda x: (0, x, 0, 0)),
        out_shape=jax.ShapeDtypeStruct((bands, planes, mine, depth), F32),
        scratch_shapes=[
            pltpu.VMEM(parts.shape, BF16),
            pltpu.VMEM((2 * bands, points), BF16),
            pltpu.VMEM(row.shape, F32),
            pltpu.SemaphoreType.DMA((2, planes // STEP)),
        ],
        compiler_params=pltpu.CompilerParams(vmem_limit_bytes=60 << 20),
        cost_estimate=cost(18 * parts.size * bands // 4, 4 * parts.size),
        name="finish",
    )(row, pair, turned, parts, early, late)


def fast(wave, direction, potential, rotation):
    bands_here, planes, rows_y, depth = wave.shape
    parts = lax.axis_size("grid")
    bands, mine = bands_here * parts, rows_y // parts
    total_x = planes * lax.axis_size("band")
    scale = [-0.5 * (n / LATTICE) ** 2 for n in (total_x, rows_y, depth)]
    weights = (
        STENCIL[0] * sum(scale),
        *([s * c for c in STENCIL[1:]] for s in scale),
    )
    ncells = total_x * rows_y * depth

    def pack(field):
        cut = field.reshape(bands_here, -1, parts, mine, depth)
        return cut.transpose(2, 0, 1, 3, 4)

    def exchange(blocks):
        got = lax.all_to_all(blocks, "grid", 0, 0, tiled=True)
        return got.reshape(bands, -1, mine, depth)

    before, after = halos(wave, "band", 1)
    w = exchange(pack(wave))
    sent, own = kinetic(wave, before, after, weights, parts)
    own = lax.dynamic_update_slice(
        jnp.zeros((bands,), F32),
        own.sum((1, 2)),
        (lax.axis_index("grid") * bands_here,),
    )
    square = w * w
    numer = own + jnp.sum(square * potential[None], axis=(1, 2, 3))
    sums = butterfly_sum(jnp.stack([numer, jnp.sum(square, axis=(1, 2, 3))]))
    t = exchange(sent)
    cut = EARLY * planes // 16
    early, late, sums, turned = lax.optimization_barrier(
        (pack(direction[:, :cut]), pack(direction[:, cut:]), sums, rotation.T)
    )
    ritz = jnp.broadcast_to((sums[0] / sums[1])[:, None], (bands, depth))
    early = exchange(early)
    pair, basis = gram_pair(t, w, potential, ritz)
    late, pair = lax.optimization_barrier((late, halved_sum(pair)))
    late = exchange(late)

    inverse = factor_pair(pair, 1.0 / ncells)
    row, early = gram_row(basis, early, jnp.zeros((2 * bands, 6 * bands), F32), 0)
    late, row, inverse = lax.optimization_barrier((late, row, inverse))
    row, late = gram_row(basis, late, row, cut)
    row = halved_sum(joined(row))
    return finish(row, inverse, turned, basis, early, late, 1.0 / ncells, mine, depth)


def axis_term(field, axis):
    total = STENCIL[0] * field
    for k in range(1, WIDTH + 1):
        total = total + STENCIL[k] * (jnp.roll(field, k, axis) + jnp.roll(field, -k, axis))
    return total


def general(wave, direction, potential, rotation):
    bands_here, planes, rows_y, depth = wave.shape
    total_x = planes * lax.axis_size("band")
    inverse_x, inverse_y, inverse_z = ((n / LATTICE) ** 2 for n in (total_x, rows_y, depth))
    before, after = halos(wave, "band", 1)
    padded = jnp.concatenate([before, wave, after], axis=1)
    along_x = STENCIL[0] * wave
    for k in range(1, WIDTH + 1):
        along_x = along_x + STENCIL[k] * (
            padded[:, WIDTH + k : WIDTH + k + planes]
            + padded[:, WIDTH - k : WIDTH - k + planes]
        )
    second = along_x * inverse_x + axis_term(wave, 2) * inverse_y + axis_term(wave, 3) * inverse_z
    local_pot = lax.all_gather(potential, "grid", axis=1, tiled=True)
    hwave = -0.5 * second + local_pot[None] * wave
    numer = jnp.sum(wave * hwave, axis=(1, 2, 3))
    denom = jnp.sum(wave * wave, axis=(1, 2, 3))
    numer, denom = lax.psum((numer, denom), "band")
    resid = hwave - (numer / denom)[:, None, None, None] * wave
    gathered = [
        lax.all_to_all(f, "grid", split_axis=2, concat_axis=0, tiled=True)
        for f in (resid, wave, direction)
    ]
    out_shape = gathered[0].shape
    stacked = jnp.concatenate(gathered, axis=0).reshape(3 * out_shape[0], -1)
    ncells = total_x * rows_y * depth
    gram = lax.psum(jnp.dot(stacked, stacked.T, precision=HIGH) / ncells, ("band", "grid"))
    factor = jnp.linalg.cholesky(gram)
    solved = jax.scipy.linalg.solve_triangular(factor, rotation, lower=True, trans=1)
    mixed = lax.dot_general(solved, stacked, (((0,), (0,)), ((), ())), precision=HIGH)
    return mixed.reshape(out_shape)


def on_device(wave, direction, potential, rotation):
    _, planes, rows_y, depth = wave.shape
    mine = rows_y // lax.axis_size("grid")
    sizes = lax.axis_size("band"), lax.axis_size("grid")
    tiled = mine == 8 and depth == 128 and planes % (8 * STEP) == 0
    tiled = tiled and all(n & (n - 1) == 0 for n in sizes) and sizes[0] > 1
    return (fast if tiled else general)(wave, direction, potential, rotation)


def solution(mesh):
    return jax.shard_map(
        on_device,
        mesh=mesh,
        in_specs=(
            P("grid", "band", None, None),
            P("grid", "band", None, None),
            P("band", "grid", None),
            P(),
        ),
        out_specs=P(None, "band", "grid", None),
        check_vma=False,
    )
```

```python
import functools

import jax
import jax.numpy as jnp
from jax import lax
from jax.experimental import pallas as pl
from jax.experimental.pallas import tpu as pltpu
from jax.sharding import PartitionSpec as P

STENCIL = (
    -5369.0 / 1800.0,
    12.0 / 7.0,
    -15.0 / 56.0,
    10.0 / 189.0,
    -1.0 / 112.0,
    2.0 / 1925.0,
    -1.0 / 16632.0,
)
LATTICE = 51.3
WIDTH = len(STENCIL) - 1
HIGH = lax.Precision.HIGHEST
F32 = jnp.float32
BF16 = jnp.bfloat16


def halos(shard, axis, dim):
    devices, length = lax.axis_size(axis), shard.shape[dim]
    up = [(i, (i + 1) % devices) for i in range(devices)]
    down = [(j, i) for i, j in up]
    last = lax.slice_in_dim(shard, length - WIDTH, length, axis=dim)
    first = lax.slice_in_dim(shard, 0, WIDTH, axis=dim)
    return lax.ppermute(last, axis, up), lax.ppermute(first, axis, down)


def butterfly_sum(value):
    for axis in ("band", "grid"):
        devices, step = lax.axis_size(axis), 1
        while step < devices:
            value = value + lax.ppermute(
                value, axis, [(i, i ^ step) for i in range(devices)]
            )
            step *= 2
    return value


def core_pairs():
    return [(i, i ^ 1) for i in range(lax.axis_size("band"))]


def half_of_sum(value):
    half, odd = value.shape[0] // 2, lax.axis_index("band") % 2 == 1
    top, bottom = value[:half], value[half:]
    mine = jnp.where(odd, bottom, top)
    mine = mine + lax.ppermute(jnp.where(odd, top, bottom), "band", core_pairs())
    bands, grids = lax.axis_size("band"), lax.axis_size("grid")
    flips = [b * grids + g for b in (0, 2) for g in (0, 1)][1:]
    got = [
        lax.ppermute(mine, ("band", "grid"), [(i, i ^ f) for i in range(bands * grids)])
        for f in flips
    ]
    mine = (mine + got[0]) + (got[1] + got[2])
    for axis, step in (("band", 4), ("grid", 2)):
        devices = lax.axis_size(axis)
        while step < devices:
            mine = mine + lax.ppermute(
                mine, axis, [(i, i ^ step) for i in range(devices)]
            )
            step *= 2
    return mine


def both_halves(mine):
    odd = lax.axis_index("band") % 2 == 1
    other = lax.ppermute(mine, "band", core_pairs())
    return jnp.concatenate([jnp.where(odd, other, mine), jnp.where(odd, mine, other)])


def kinetic_kernel(weights, w_ref, lo_ref, hi_ref, t_ref, s_ref, pad):
    _, planes, rows, depth = w_ref.shape
    parts, _, _, mine, _ = t_ref.shape
    center, along_x, along_y, along_z = weights
    pad[0:WIDTH] = lo_ref[0]
    pad[WIDTH : WIDTH + planes] = w_ref[0]
    pad[WIDTH + planes :] = hi_ref[0]

    def plane(i, total):
        here = pad[i + WIDTH]
        out = center * here
        for k in range(1, WIDTH + 1):
            out += along_x[k - 1] * (pad[i + WIDTH + k] + pad[i + WIDTH - k])
            out += along_y[k - 1] * (
                pltpu.roll(here, k, 0) + pltpu.roll(here, rows - k, 0)
            )
            out += along_z[k - 1] * (
                pltpu.roll(here, k, 1) + pltpu.roll(here, depth - k, 1)
            )
        t_ref[:, 0, i] = out.reshape(parts, mine, depth)
        return total + (here * out).reshape(-1, 8, depth).sum(0)

    s_ref[0] = lax.fori_loop(0, planes, plane, jnp.zeros((8, depth), F32))


def kinetic(wave, before, after, weights, parts):
    bands, planes, rows, depth = wave.shape
    spec = lambda n: pl.BlockSpec((1, n, rows, depth), lambda b: (b, 0, 0, 0))
    return pl.pallas_call(
        functools.partial(kinetic_kernel, weights),
        grid=(bands,),
        in_specs=[spec(planes), spec(WIDTH), spec(WIDTH)],
        out_specs=[
            pl.BlockSpec(
                (parts, 1, planes, rows // parts, depth), lambda b: (0, b, 0, 0, 0)
            ),
            pl.BlockSpec((1, 8, depth), lambda b: (b, 0, 0)),
        ],
        out_shape=[
            jax.ShapeDtypeStruct((parts, bands, planes, rows // parts, depth), F32),
            jax.ShapeDtypeStruct((bands, 8, depth), F32),
        ],
        scratch_shapes=[pltpu.VMEM((planes + 2 * WIDTH, rows, depth), F32)],
        compiler_params=pltpu.CompilerParams(vmem_limit_bytes=32 << 20),
        cost_estimate=pl.CostEstimate(
            flops=60 * wave.size, bytes_accessed=11 * wave.size, transcendentals=0
        ),
        name="kinetic",
    )(wave, before, after)


def split(value):
    high = value.astype(BF16)
    return high, (value - high.astype(F32)).astype(BF16)


def dot_t(a, b, precision=None):
    return lax.dot_general(
        a, b, (((1,), (1,)), ((), ())), precision=precision, preferred_element_type=F32
    )


def dot(a, b, precision=None):
    return jnp.dot(a, b, precision=precision, preferred_element_type=F32)


def row_of(ref, i):
    bands, planes, mine, depth = ref.shape
    flat = ref.reshape(bands * planes * mine, depth)
    return flat[pl.ds(i, bands, stride=planes * mine), :]


def split_rows(ref):
    count = ref.shape[1] * ref.shape[2]
    highs, lows = zip(*(split(row_of(ref, i)) for i in range(count)))
    return jnp.concatenate(highs, axis=1), jnp.concatenate(lows, axis=1)


def gram_pair_kernel(t_ref, w_ref, v_ref, ritz_ref, g_ref, parts_ref, acc, cross):
    step, last = pl.program_id(0), pl.num_programs(0) - 1
    bands, planes, mine, depth = w_ref.shape

    @pl.when(step == 0)
    def _():
        acc[...] = jnp.zeros_like(acc)
        cross[...] = jnp.zeros_like(cross)

    for i in range(planes * mine):
        w = row_of(w_ref, i)
        x, y = i // mine, i % mine
        r = row_of(t_ref, i) + (v_ref[x, y : y + 1, :] - ritz_ref[...]) * w
        high, low = split(jnp.concatenate([r, w], axis=0))
        parts_ref[: 2 * bands, i * depth : (i + 1) * depth] = high
        parts_ref[2 * bands :, i * depth : (i + 1) * depth] = low
    high = parts_ref[: 2 * bands]
    acc[...] += dot_t(high, high)
    cross[...] += dot_t(high, parts_ref[2 * bands :])

    @pl.when(step == last)
    def _():
        g_ref[...] = acc[...] + (cross[...] + cross[...].T)


def gram_row_kernel(parts_ref, d_ref, g_ref, both_hbm, held, sems):
    step, last = pl.program_id(0), pl.num_programs(0) - 1
    points, count = parts_ref.shape

    @pl.when(step == 0)
    def _():
        g_ref[...] = jnp.zeros_like(g_ref)

    def copy_of(at):
        to = both_hbm.at[:, pl.ds(pl.multiple_of(at * count, count), count)]
        return pltpu.make_async_copy(held.at[at % 2], to, sems.at[at % 2])

    @pl.when(step >= 2)
    def _():
        copy_of(step - 2).wait()

    both = jnp.concatenate(split_rows(d_ref), axis=0)
    held[step % 2] = both
    copy_of(step).start()
    g_ref[:, :points] += dot_t(both, parts_ref[...])
    g_ref[:, points:] += dot_t(both, both)

    @pl.when(step == last)
    def _():
        copy_of(step - 1).wait()
        copy_of(step).wait()


def apply_points(parts, both, c_ref, o_ref):
    bands, planes, mine, depth = o_ref.shape
    high, low = split(c_ref[...])
    pair, last = slice(0, 2 * bands), slice(2 * bands, 3 * bands)
    stacked = jnp.concatenate([high[:, pair], low[:, pair]], axis=0)
    ending = jnp.concatenate(
        [
            jnp.concatenate([high[:, last], high[:, last]], axis=1),
            jnp.concatenate([low[:, last], jnp.zeros_like(low[:, last])], axis=1),
        ],
        axis=0,
    )
    wide = dot(stacked, parts[: 2 * bands]) + dot(ending, both)
    out = wide[:bands] + wide[bands:] + dot(high[:, pair], parts[2 * bands :])
    flat = o_ref.reshape(bands * planes * mine, depth)
    for i in range(planes * mine):
        flat[pl.ds(i, bands, stride=planes * mine), :] = out[:, i * depth : (i + 1) * depth]


def tile_spec(bands, planes, mine, depth):
    return pl.BlockSpec((bands, planes, mine, depth), lambda x: (0, x, 0, 0))


def cost(flops, nbytes):
    return pl.CostEstimate(flops=flops, bytes_accessed=nbytes, transcendentals=0)


STEP = 2
EARLY = 12


def gram_pair(t, w, v, ritz):
    bands, planes, mine, depth = w.shape
    tile = tile_spec(bands, STEP, mine, depth)
    points = pl.BlockSpec((4 * bands, STEP * mine * depth), lambda x: (0, x))
    parts = jax.ShapeDtypeStruct((4 * bands, planes * mine * depth), BF16)
    square = (2 * bands, 2 * bands)
    return pl.pallas_call(
        gram_pair_kernel,
        grid=(planes // STEP,),
        in_specs=[
            tile,
            tile,
            pl.BlockSpec((STEP, mine, depth), lambda x: (x, 0, 0)),
            pl.BlockSpec((bands, depth), lambda x: (0, 0)),
        ],
        out_specs=[pl.BlockSpec(square, lambda x: (0, 0)), points],
        out_shape=[jax.ShapeDtypeStruct(square, F32), parts],
        scratch_shapes=[pltpu.VMEM(square, F32), pltpu.VMEM(square, F32)],
        compiler_params=pltpu.CompilerParams(vmem_limit_bytes=60 << 20),
        cost_estimate=cost(16 * bands * w.size, 16 * w.size),
        name="gram_pair",
    )(t, w, v, ritz)


def gram_row(parts, d, skip):
    bands, planes, mine, depth = d.shape
    count = STEP * mine * depth
    shape = (2 * bands, 6 * bands)
    products, both = pl.pallas_call(
        gram_row_kernel,
        grid=(planes // STEP,),
        in_specs=[
            pl.BlockSpec((4 * bands, count), lambda x: (0, x + skip // STEP)),
            tile_spec(bands, STEP, mine, depth),
        ],
        out_specs=[
            pl.BlockSpec(shape, lambda x: (0, 0)),
            pl.BlockSpec(memory_space=pltpu.HBM),
        ],
        out_shape=[
            jax.ShapeDtypeStruct(shape, F32),
            jax.ShapeDtypeStruct((2 * bands, planes * mine * depth), BF16),
        ],
        scratch_shapes=[
            pltpu.VMEM((2, 2 * bands, count), BF16),
            pltpu.SemaphoreType.DMA((2,)),
        ],
        compiler_params=pltpu.CompilerParams(vmem_limit_bytes=(60 if skip == 0 else 40) << 20),
        cost_estimate=cost(18 * bands * d.size, 12 * d.size),
        name="gram_row",
    )(parts, d)
    wide = products[:bands] + products[bands:]
    pair = wide[:, : 2 * bands] + wide[:, 2 * bands : 4 * bands]
    own = wide[:, 4 * bands : 5 * bands] + wide[:, 5 * bands :]
    return jnp.concatenate([pair, own], axis=1), both


def spread_row(value, i):
    return jnp.broadcast_to(value[i : i + 1, :], value.shape)


def spread_column(value, j):
    return jnp.broadcast_to(value[:, j : j + 1], value.shape)


def inverse_factor(matrix):
    size = matrix.shape[0]
    count = size // 8
    shape = (8, size)
    sublane = lax.broadcasted_iota(jnp.int32, shape, 0)
    lane = lax.broadcasted_iota(jnp.int32, shape, 1)
    left = [matrix[8 * q : 8 * q + 8] for q in range(count)]
    right = [jnp.where(lane == sublane + 8 * q, 1.0, 0.0).astype(F32) for q in range(count)]
    done = []
    for p in range(count):
        base = 8 * p
        rows = [spread_row(left[p], i) for i in range(8)]
        ones = [spread_row(right[p], i) for i in range(8)]
        entry = {
            (i, j): spread_column(rows[i], base + j) for i in range(8) for j in range(i, 8)
        }
        unit, inverse = {}, []
        for k in range(8):
            inverse.append(1.0 / entry[k, k])
            for i in range(k + 1, 8):
                unit[i, k] = entry[k, i] * inverse[k]
            for i in range(k + 1, 8):
                for j in range(i, 8):
                    entry[i, j] = entry[i, j] - unit[i, k] * entry[k, j]
        for i in range(8):
            for k in range(i):
                rows[i] = rows[i] - unit[i, k] * rows[k]
                ones[i] = ones[i] - unit[i, k] * ones[k]
        out = ones[0] * lax.rsqrt(entry[0, 0])
        for i in range(1, 8):
            out = jnp.where(sublane == i, ones[i] * lax.rsqrt(entry[i, i]), out)
        done.append(out)
        if p == count - 1:
            break
        for i in reversed(range(8)):
            rows[i] = rows[i] * inverse[i]
            ones[i] = ones[i] * inverse[i]
            for k in range(i + 1, 8):
                rows[i] = rows[i] - unit[k, i] * rows[k]
                ones[i] = ones[i] - unit[k, i] * ones[k]
        for q in range(p + 1, count):
            columns = [spread_column(left[q], base + i) for i in range(8)]
            for i in range(8):
                left[q] = left[q] - columns[i] * rows[i]
                right[q] = right[q] - columns[i] * ones[i]
    return jnp.concatenate(done, axis=0)


def factor_first_kernel(scale, g_ref, o_ref):
    o_ref[...] = inverse_factor(g_ref[...] * scale)


def factor_second_kernel(scale, g_ref, first_ref, o_ref):
    half = first_ref.shape[0]
    first = first_ref[...]
    lower = dot_t(g_ref[:, :half] * scale, first, HIGH)
    second = inverse_factor(g_ref[:, half:] * scale - dot_t(lower, lower, HIGH))
    o_ref[:half, :half] = first
    o_ref[:half, half:] = jnp.zeros((half, half), F32)
    o_ref[half:, :half] = -dot(second, dot(lower, first, HIGH), HIGH)
    o_ref[half:, half:] = second


def factor_pair(gram, scale):
    half = gram.shape[0] // 2
    first = pl.pallas_call(
        functools.partial(factor_first_kernel, scale),
        grid=(1,),
        in_specs=[pl.BlockSpec((half, half), lambda i: (0, 0))],
        out_specs=pl.BlockSpec((half, half), lambda i: (0, 0)),
        out_shape=jax.ShapeDtypeStruct((half, half), F32),
        cost_estimate=cost(10**9, gram.size),
        name="factor_first",
    )(gram)
    return pl.pallas_call(
        functools.partial(factor_second_kernel, scale),
        grid=(1,),
        in_specs=[
            pl.BlockSpec((half, 2 * half), lambda i: (1, 0)),
            pl.BlockSpec((half, half), lambda i: (0, 0)),
        ],
        out_specs=pl.BlockSpec((2 * half, 2 * half), lambda i: (0, 0)),
        out_shape=jax.ShapeDtypeStruct(gram.shape, F32),
        cost_estimate=cost(10**9, 4 * gram.size),
        name="factor_second",
    )(gram, first)


def finish_kernel(scale, row_ref, pair_ref, turned_ref, parts_hbm, early_hbm, late_hbm, o_ref, *scratch):
    parts_ref, both_ref, c_ref, sems = scratch
    step, bands = pl.program_id(0), row_ref.shape[0]
    count = parts_ref.shape[1] // pl.num_programs(0)
    cut = early_hbm.shape[1] // count

    @pl.when(step == 0)
    def _():
        for i in range(parts_ref.shape[1] // count):
            to = pl.ds(i * count, count)
            d_hbm, at = (early_hbm, i) if i < cut else (late_hbm, i - cut)
            own = d_hbm.at[:, pl.ds(at * count, count)]
            pltpu.make_async_copy(parts_hbm.at[:, to], parts_ref.at[:, to], sems.at[0, i]).start()
            pltpu.make_async_copy(own, both_ref.at[:, to], sems.at[1, i]).start()
        pair = pair_ref[...]
        lower = dot_t(row_ref[:, : 2 * bands] * scale, pair, HIGH)
        last = inverse_factor(row_ref[:, 2 * bands :] * scale - dot_t(lower, lower, HIGH))
        tail = dot(turned_ref[:, 2 * bands :], last, HIGH)
        c_ref[:, 2 * bands :] = tail
        rest = turned_ref[:, : 2 * bands] - dot(tail, lower, HIGH)
        c_ref[:, : 2 * bands] = dot(rest, pair, HIGH)

    here = pl.ds(pl.multiple_of(step * count, count), count)
    for to_ref, sem in ((parts_ref, sems.at[0, step]), (both_ref, sems.at[1, step])):
        pltpu.make_async_copy(to_ref.at[:, here], to_ref.at[:, here], sem).wait()
    apply_points(parts_ref[:, here], both_ref[:, here], c_ref, o_ref)


def finish(row, pair, turned, parts, early, late, scale, mine, depth):
    bands, points = row.shape[0], parts.shape[1]
    planes = points // (mine * depth)
    far = pl.BlockSpec(memory_space=pl.ANY)
    whole = lambda a: pl.BlockSpec(a.shape, lambda x: (0, 0), pipeline_mode=pl.Buffered(1))
    return pl.pallas_call(
        functools.partial(finish_kernel, scale),
        grid=(planes // STEP,),
        in_specs=[whole(row), whole(pair), whole(turned), far, far, far],
        out_specs=pl.BlockSpec((bands, STEP, mine, depth), lambda x: (0, x, 0, 0)),
        out_shape=jax.ShapeDtypeStruct((bands, planes, mine, depth), F32),
        scratch_shapes=[
            pltpu.VMEM(parts.shape, BF16),
            pltpu.VMEM((2 * bands, points), BF16),
            pltpu.VMEM(row.shape, F32),
            pltpu.SemaphoreType.DMA((2, planes // STEP)),
        ],
        compiler_params=pltpu.CompilerParams(vmem_limit_bytes=60 << 20),
        cost_estimate=cost(18 * parts.size * bands // 4, 4 * parts.size),
        name="finish",
    )(row, pair, turned, parts, early, late)


def fast(wave, direction, potential, rotation):
    bands_here, planes, rows_y, depth = wave.shape
    parts = lax.axis_size("grid")
    bands, mine = bands_here * parts, rows_y // parts
    total_x = planes * lax.axis_size("band")
    scale = [-0.5 * (n / LATTICE) ** 2 for n in (total_x, rows_y, depth)]
    weights = (
        STENCIL[0] * sum(scale),
        *([s * c for c in STENCIL[1:]] for s in scale),
    )
    ncells = total_x * rows_y * depth

    def pack(field):
        cut = field.reshape(bands_here, -1, parts, mine, depth)
        return cut.transpose(2, 0, 1, 3, 4)

    def exchange(blocks):
        got = lax.all_to_all(blocks, "grid", 0, 0, tiled=True)
        return got.reshape(bands, -1, mine, depth)

    before, after = halos(wave, "band", 1)
    w = exchange(pack(wave))
    sent, own = kinetic(wave, before, after, weights, parts)
    own = lax.dynamic_update_slice(
        jnp.zeros((bands,), F32),
        own.sum((1, 2)),
        (lax.axis_index("grid") * bands_here,),
    )
    square = w * w
    numer = own + jnp.sum(square * potential[None], axis=(1, 2, 3))
    sums = butterfly_sum(jnp.stack([numer, jnp.sum(square, axis=(1, 2, 3))]))
    t = exchange(sent)
    cut = EARLY * planes // 16
    early, late, sums, turned = lax.optimization_barrier(
        (pack(direction[:, :cut]), pack(direction[:, cut:]), sums, rotation.T)
    )
    ritz = jnp.broadcast_to((sums[0] / sums[1])[:, None], (bands, depth))
    early = exchange(early)
    pair, basis = gram_pair(t, w, potential, ritz)
    late, half = lax.optimization_barrier((late, half_of_sum(pair)))
    late = exchange(late)
    pair = both_halves(half)

    inverse = factor_pair(pair, 1.0 / ncells)
    row, early = gram_row(basis, early, 0)
    late, row, inverse = lax.optimization_barrier((late, row, inverse))
    late_row, late = gram_row(basis, late, cut)
    row = both_halves(half_of_sum(row + late_row))
    return finish(row, inverse, turned, basis, early, late, 1.0 / ncells, mine, depth)


def axis_term(field, axis):
    total = STENCIL[0] * field
    for k in range(1, WIDTH + 1):
        total = total + STENCIL[k] * (jnp.roll(field, k, axis) + jnp.roll(field, -k, axis))
    return total


def general(wave, direction, potential, rotation):
    bands_here, planes, rows_y, depth = wave.shape
    total_x = planes * lax.axis_size("band")
    inverse_x, inverse_y, inverse_z = ((n / LATTICE) ** 2 for n in (total_x, rows_y, depth))
    before, after = halos(wave, "band", 1)
    padded = jnp.concatenate([before, wave, after], axis=1)
    along_x = STENCIL[0] * wave
    for k in range(1, WIDTH + 1):
        along_x = along_x + STENCIL[k] * (
            padded[:, WIDTH + k : WIDTH + k + planes]
            + padded[:, WIDTH - k : WIDTH - k + planes]
        )
    second = along_x * inverse_x + axis_term(wave, 2) * inverse_y + axis_term(wave, 3) * inverse_z
    local_pot = lax.all_gather(potential, "grid", axis=1, tiled=True)
    hwave = -0.5 * second + local_pot[None] * wave
    numer = jnp.sum(wave * hwave, axis=(1, 2, 3))
    denom = jnp.sum(wave * wave, axis=(1, 2, 3))
    numer, denom = lax.psum((numer, denom), "band")
    resid = hwave - (numer / denom)[:, None, None, None] * wave
    gathered = [
        lax.all_to_all(f, "grid", split_axis=2, concat_axis=0, tiled=True)
        for f in (resid, wave, direction)
    ]
    out_shape = gathered[0].shape
    stacked = jnp.concatenate(gathered, axis=0).reshape(3 * out_shape[0], -1)
    ncells = total_x * rows_y * depth
    gram = lax.psum(jnp.dot(stacked, stacked.T, precision=HIGH) / ncells, ("band", "grid"))
    factor = jnp.linalg.cholesky(gram)
    solved = jax.scipy.linalg.solve_triangular(factor, rotation, lower=True, trans=1)
    mixed = lax.dot_general(solved, stacked, (((0,), (0,)), ((), ())), precision=HIGH)
    return mixed.reshape(out_shape)


def on_device(wave, direction, potential, rotation):
    _, planes, rows_y, depth = wave.shape
    mine = rows_y // lax.axis_size("grid")
    sizes = lax.axis_size("band"), lax.axis_size("grid")
    tiled = mine == 8 and depth == 128 and planes % (8 * STEP) == 0
    tiled = tiled and all(n & (n - 1) == 0 for n in sizes) and sizes[0] >= 4
    return (fast if tiled else general)(wave, direction, potential, rotation)


def solution(mesh):
    return jax.shard_map(
        on_device,
        mesh=mesh,
        in_specs=(
            P("grid", "band", None, None),
            P("grid", "band", None, None),
            P("band", "grid", None),
            P(),
        ),
        out_specs=P(None, "band", "grid", None),
        check_vma=False,
    )
```

```python
import functools

import jax
import jax.numpy as jnp
from jax import lax
from jax.experimental import pallas as pl
from jax.experimental.pallas import tpu as pltpu
from jax.sharding import PartitionSpec as P

STENCIL = (
    -5369.0 / 1800.0,
    12.0 / 7.0,
    -15.0 / 56.0,
    10.0 / 189.0,
    -1.0 / 112.0,
    2.0 / 1925.0,
    -1.0 / 16632.0,
)
LATTICE = 51.3
WIDTH = len(STENCIL) - 1
HIGH = lax.Precision.HIGHEST
F32 = jnp.float32
BF16 = jnp.bfloat16


def halos(shard, axis, dim):
    devices, length = lax.axis_size(axis), shard.shape[dim]
    up = [(i, (i + 1) % devices) for i in range(devices)]
    down = [(j, i) for i, j in up]
    last = lax.slice_in_dim(shard, length - WIDTH, length, axis=dim)
    first = lax.slice_in_dim(shard, 0, WIDTH, axis=dim)
    return lax.ppermute(last, axis, up), lax.ppermute(first, axis, down)


def butterfly_sum(value):
    for axis in ("band", "grid"):
        devices, step = lax.axis_size(axis), 1
        while step < devices:
            value = value + lax.ppermute(
                value, axis, [(i, i ^ step) for i in range(devices)]
            )
            step *= 2
    return value


def core_pairs():
    return [(i, i ^ 1) for i in range(lax.axis_size("band"))]


def half_of_sum(value):
    half, odd = value.shape[0] // 2, lax.axis_index("band") % 2 == 1
    top, bottom = value[:half], value[half:]
    mine = jnp.where(odd, bottom, top)
    mine = mine + lax.ppermute(jnp.where(odd, top, bottom), "band", core_pairs())
    bands, grids = lax.axis_size("band"), lax.axis_size("grid")
    flips = [b * grids + g for b in (0, 2) for g in (0, 1)][1:]
    got = [
        lax.ppermute(mine, ("band", "grid"), [(i, i ^ f) for i in range(bands * grids)])
        for f in flips
    ]
    mine = (mine + got[0]) + (got[1] + got[2])
    for axis, step in (("band", 4), ("grid", 2)):
        devices = lax.axis_size(axis)
        while step < devices:
            mine = mine + lax.ppermute(
                mine, axis, [(i, i ^ step) for i in range(devices)]
            )
            step *= 2
    return mine


def both_halves(mine):
    odd = lax.axis_index("band") % 2 == 1
    other = lax.ppermute(mine, "band", core_pairs())
    return jnp.concatenate([jnp.where(odd, other, mine), jnp.where(odd, mine, other)])


def kinetic_kernel(weights, w_ref, lo_ref, hi_ref, t_ref, s_ref, pad):
    _, planes, rows, depth = w_ref.shape
    parts, _, _, mine, _ = t_ref.shape
    center, along_x, along_y, along_z = weights
    pad[0:WIDTH] = lo_ref[0]
    pad[WIDTH : WIDTH + planes] = w_ref[0]
    pad[WIDTH + planes :] = hi_ref[0]

    def plane(i, total):
        here = pad[i + WIDTH]
        out = center * here
        for k in range(1, WIDTH + 1):
            out += along_x[k - 1] * (pad[i + WIDTH + k] + pad[i + WIDTH - k])
            out += along_y[k - 1] * (
                pltpu.roll(here, k, 0) + pltpu.roll(here, rows - k, 0)
            )
            out += along_z[k - 1] * (
                pltpu.roll(here, k, 1) + pltpu.roll(here, depth - k, 1)
            )
        t_ref[:, 0, i] = out.reshape(parts, mine, depth)
        return total + (here * out).reshape(-1, 8, depth).sum(0)

    s_ref[0] = lax.fori_loop(0, planes, plane, jnp.zeros((8, depth), F32))


def kinetic(wave, before, after, weights, parts):
    bands, planes, rows, depth = wave.shape
    spec = lambda n: pl.BlockSpec((1, n, rows, depth), lambda b: (b, 0, 0, 0))
    return pl.pallas_call(
        functools.partial(kinetic_kernel, weights),
        grid=(bands,),
        in_specs=[spec(planes), spec(WIDTH), spec(WIDTH)],
        out_specs=[
            pl.BlockSpec(
                (parts, 1, planes, rows // parts, depth), lambda b: (0, b, 0, 0, 0)
            ),
            pl.BlockSpec((1, 8, depth), lambda b: (b, 0, 0)),
        ],
        out_shape=[
            jax.ShapeDtypeStruct((parts, bands, planes, rows // parts, depth), F32),
            jax.ShapeDtypeStruct((bands, 8, depth), F32),
        ],
        scratch_shapes=[pltpu.VMEM((planes + 2 * WIDTH, rows, depth), F32)],
        compiler_params=pltpu.CompilerParams(vmem_limit_bytes=32 << 20),
        cost_estimate=pl.CostEstimate(
            flops=60 * wave.size, bytes_accessed=11 * wave.size, transcendentals=0
        ),
        name="kinetic",
    )(wave, before, after)


def split(value):
    high = value.astype(BF16)
    return high, (value - high.astype(F32)).astype(BF16)


def dot_t(a, b, precision=None):
    return lax.dot_general(
        a, b, (((1,), (1,)), ((), ())), precision=precision, preferred_element_type=F32
    )


def dot(a, b, precision=None):
    return jnp.dot(a, b, precision=precision, preferred_element_type=F32)


def row_of(ref, i):
    bands, planes, mine, depth = ref.shape
    flat = ref.reshape(bands * planes * mine, depth)
    return flat[pl.ds(i, bands, stride=planes * mine), :]


def split_rows(ref):
    count = ref.shape[1] * ref.shape[2]
    highs, lows = zip(*(split(row_of(ref, i)) for i in range(count)))
    return jnp.concatenate(highs, axis=1), jnp.concatenate(lows, axis=1)


def gram_pair_kernel(t_ref, w_ref, v_ref, ritz_ref, g_ref, parts_ref, acc, cross):
    step, last = pl.program_id(0), pl.num_programs(0) - 1
    bands, planes, mine, depth = w_ref.shape

    @pl.when(step == 0)
    def _():
        acc[...] = jnp.zeros_like(acc)
        cross[...] = jnp.zeros_like(cross)

    for i in range(planes * mine):
        w = row_of(w_ref, i)
        x, y = i // mine, i % mine
        r = row_of(t_ref, i) + (v_ref[x, y : y + 1, :] - ritz_ref[...]) * w
        high, low = split(jnp.concatenate([r, w], axis=0))
        parts_ref[: 2 * bands, i * depth : (i + 1) * depth] = high
        parts_ref[2 * bands :, i * depth : (i + 1) * depth] = low
    high = parts_ref[: 2 * bands]
    acc[...] += dot_t(high, high)
    cross[...] += dot_t(high, parts_ref[2 * bands :])

    @pl.when(step == last)
    def _():
        g_ref[...] = acc[...] + (cross[...] + cross[...].T)


def gram_row_kernel(parts_ref, d_ref, g_ref, both_hbm, held, sems):
    step, last = pl.program_id(0), pl.num_programs(0) - 1
    points, count = parts_ref.shape

    @pl.when(step == 0)
    def _():
        g_ref[...] = jnp.zeros_like(g_ref)

    def copy_of(at):
        to = both_hbm.at[:, pl.ds(pl.multiple_of(at * count, count), count)]
        return pltpu.make_async_copy(held.at[at % 2], to, sems.at[at % 2])

    @pl.when(step >= 2)
    def _():
        copy_of(step - 2).wait()

    both = jnp.concatenate(split_rows(d_ref), axis=0)
    held[step % 2] = both
    copy_of(step).start()
    g_ref[:, :points] += dot_t(both, parts_ref[...])
    g_ref[:, points:] += dot_t(both, both)

    @pl.when(step == last)
    def _():
        copy_of(step - 1).wait()
        copy_of(step).wait()


def apply_points(parts, both, c_ref, o_ref):
    bands, planes, mine, depth = o_ref.shape
    high, low = split(c_ref[...])
    pair, last = slice(0, 2 * bands), slice(2 * bands, 3 * bands)
    stacked = jnp.concatenate([high[:, pair], low[:, pair]], axis=0)
    ending = jnp.concatenate(
        [
            jnp.concatenate([high[:, last], high[:, last]], axis=1),
            jnp.concatenate([low[:, last], jnp.zeros_like(low[:, last])], axis=1),
        ],
        axis=0,
    )
    wide = dot(stacked, parts[: 2 * bands]) + dot(ending, both)
    out = wide[:bands] + wide[bands:] + dot(high[:, pair], parts[2 * bands :])
    flat = o_ref.reshape(bands * planes * mine, depth)
    for i in range(planes * mine):
        flat[pl.ds(i, bands, stride=planes * mine), :] = out[:, i * depth : (i + 1) * depth]


def tile_spec(bands, planes, mine, depth):
    return pl.BlockSpec((bands, planes, mine, depth), lambda x: (0, x, 0, 0))


def cost(flops, nbytes):
    return pl.CostEstimate(flops=flops, bytes_accessed=nbytes, transcendentals=0)


STEP = 2
EARLY = 12


def gram_pair(t, w, v, ritz):
    bands, planes, mine, depth = w.shape
    tile = tile_spec(bands, STEP, mine, depth)
    points = pl.BlockSpec((4 * bands, STEP * mine * depth), lambda x: (0, x))
    parts = jax.ShapeDtypeStruct((4 * bands, planes * mine * depth), BF16)
    square = (2 * bands, 2 * bands)
    return pl.pallas_call(
        gram_pair_kernel,
        grid=(planes // STEP,),
        in_specs=[
            tile,
            tile,
            pl.BlockSpec((STEP, mine, depth), lambda x: (x, 0, 0)),
            pl.BlockSpec((bands, depth), lambda x: (0, 0)),
        ],
        out_specs=[pl.BlockSpec(square, lambda x: (0, 0)), points],
        out_shape=[jax.ShapeDtypeStruct(square, F32), parts],
        scratch_shapes=[pltpu.VMEM(square, F32), pltpu.VMEM(square, F32)],
        compiler_params=pltpu.CompilerParams(vmem_limit_bytes=60 << 20),
        cost_estimate=cost(16 * bands * w.size, 16 * w.size),
        name="gram_pair",
    )(t, w, v, ritz)


def gram_row(parts, d, skip):
    bands, planes, mine, depth = d.shape
    count = STEP * mine * depth
    shape = (2 * bands, 6 * bands)
    products, both = pl.pallas_call(
        gram_row_kernel,
        grid=(planes // STEP,),
        in_specs=[
            pl.BlockSpec((4 * bands, count), lambda x: (0, x + skip // STEP)),
            tile_spec(bands, STEP, mine, depth),
        ],
        out_specs=[
            pl.BlockSpec(shape, lambda x: (0, 0)),
            pl.BlockSpec(memory_space=pltpu.HBM),
        ],
        out_shape=[
            jax.ShapeDtypeStruct(shape, F32),
            jax.ShapeDtypeStruct((2 * bands, planes * mine * depth), BF16),
        ],
        scratch_shapes=[
            pltpu.VMEM((2, 2 * bands, count), BF16),
            pltpu.SemaphoreType.DMA((2,)),
        ],
        compiler_params=pltpu.CompilerParams(vmem_limit_bytes=(60 if skip == 0 else 40) << 20),
        cost_estimate=cost(18 * bands * d.size, 12 * d.size),
        name="gram_row",
    )(parts, d)
    wide = products[:bands] + products[bands:]
    pair = wide[:, : 2 * bands] + wide[:, 2 * bands : 4 * bands]
    own = wide[:, 4 * bands : 5 * bands] + wide[:, 5 * bands :]
    return jnp.concatenate([pair, own], axis=1), both


def spread_row(value, i):
    return jnp.broadcast_to(value[i : i + 1, :], value.shape)


def spread_column(value, j):
    return jnp.broadcast_to(value[:, j : j + 1], value.shape)


def inverse_factor(matrix):
    size = matrix.shape[0]
    count = size // 8
    shape = (8, size)
    sublane = lax.broadcasted_iota(jnp.int32, shape, 0)
    lane = lax.broadcasted_iota(jnp.int32, shape, 1)
    blocks = [matrix[8 * q : 8 * q + 8] for q in range(count)]
    done = []
    for p in range(count):
        base = 8 * p
        own = (lane >= base) & (lane < base + 8)
        rows = [spread_row(blocks[p], i) for i in range(8)]
        entry = {
            (i, j): spread_column(rows[i], base + j) for i in range(8) for j in range(i, 8)
        }
        unit, inverse = {}, []
        for k in range(8):
            inverse.append(1.0 / entry[k, k])
            for i in range(k + 1, 8):
                unit[i, k] = entry[k, i] * inverse[k]
            for i in range(k + 1, 8):
                for j in range(i, 8):
                    entry[i, j] = entry[i, j] - unit[i, k] * entry[k, j]
        for i in range(8):
            rows[i] = jnp.where(own, jnp.where(lane == base + i, 1.0, 0.0), rows[i])
            for k in range(i):
                rows[i] = rows[i] - unit[i, k] * rows[k]
        out = rows[0] * lax.rsqrt(entry[0, 0])
        for i in range(1, 8):
            out = jnp.where(sublane == i, rows[i] * lax.rsqrt(entry[i, i]), out)
        done.append(jnp.where(lane < base + 8, out, 0.0))
        if p == count - 1:
            break
        for i in reversed(range(8)):
            rows[i] = rows[i] * inverse[i]
            for k in reversed(range(i + 1, 8)):
                rows[i] = rows[i] - unit[k, i] * rows[k]
        for q in range(p + 1, count):
            columns = [spread_column(blocks[q], base + i) for i in range(8)]
            blocks[q] = jnp.where(own, 0.0, blocks[q])
            for i in reversed(range(8)):
                blocks[q] = blocks[q] - columns[i] * rows[i]
    return jnp.concatenate(done, axis=0)


def factor_first_kernel(scale, g_ref, o_ref):
    o_ref[...] = inverse_factor(g_ref[...] * scale)


def factor_second_kernel(scale, g_ref, first_ref, o_ref):
    half = first_ref.shape[0]
    first = first_ref[...]
    lower = dot_t(g_ref[:, :half] * scale, first, HIGH)
    second = inverse_factor(g_ref[:, half:] * scale - dot_t(lower, lower, HIGH))
    o_ref[:half, :half] = first
    o_ref[:half, half:] = jnp.zeros((half, half), F32)
    o_ref[half:, :half] = -dot(second, dot(lower, first, HIGH), HIGH)
    o_ref[half:, half:] = second


def factor_pair(gram, scale):
    half = gram.shape[0] // 2
    first = pl.pallas_call(
        functools.partial(factor_first_kernel, scale),
        grid=(1,),
        in_specs=[pl.BlockSpec((half, half), lambda i: (0, 0))],
        out_specs=pl.BlockSpec((half, half), lambda i: (0, 0)),
        out_shape=jax.ShapeDtypeStruct((half, half), F32),
        cost_estimate=cost(10**9, gram.size),
        name="factor_first",
    )(gram)
    return pl.pallas_call(
        functools.partial(factor_second_kernel, scale),
        grid=(1,),
        in_specs=[
            pl.BlockSpec((half, 2 * half), lambda i: (1, 0)),
            pl.BlockSpec((half, half), lambda i: (0, 0)),
        ],
        out_specs=pl.BlockSpec((2 * half, 2 * half), lambda i: (0, 0)),
        out_shape=jax.ShapeDtypeStruct(gram.shape, F32),
        cost_estimate=cost(10**9, 4 * gram.size),
        name="factor_second",
    )(gram, first)


def finish_kernel(scale, row_ref, pair_ref, turned_ref, parts_hbm, early_hbm, late_hbm, o_ref, *scratch):
    parts_ref, both_ref, c_ref, sems = scratch
    step, bands = pl.program_id(0), row_ref.shape[0]
    count = parts_ref.shape[1] // pl.num_programs(0)
    cut = early_hbm.shape[1] // count

    @pl.when(step == 0)
    def _():
        for i in range(parts_ref.shape[1] // count):
            to = pl.ds(i * count, count)
            d_hbm, at = (early_hbm, i) if i < cut else (late_hbm, i - cut)
            own = d_hbm.at[:, pl.ds(at * count, count)]
            pltpu.make_async_copy(parts_hbm.at[:, to], parts_ref.at[:, to], sems.at[0, i]).start()
            pltpu.make_async_copy(own, both_ref.at[:, to], sems.at[1, i]).start()
        pair = pair_ref[...]
        lower = dot_t(row_ref[:, : 2 * bands] * scale, pair, HIGH)
        last = inverse_factor(row_ref[:, 2 * bands :] * scale - dot_t(lower, lower, HIGH))
        first, through = dot(turned_ref[:, : 2 * bands], pair, HIGH), dot(lower, pair, HIGH)
        tail = dot(turned_ref[:, 2 * bands :], last, HIGH)
        c_ref[:, 2 * bands :] = tail
        c_ref[:, : 2 * bands] = first - dot(tail, through, HIGH)

    here = pl.ds(pl.multiple_of(step * count, count), count)
    for to_ref, sem in ((parts_ref, sems.at[0, step]), (both_ref, sems.at[1, step])):
        pltpu.make_async_copy(to_ref.at[:, here], to_ref.at[:, here], sem).wait()
    apply_points(parts_ref[:, here], both_ref[:, here], c_ref, o_ref)


def finish(row, pair, turned, parts, early, late, scale, mine, depth):
    bands, points = row.shape[0], parts.shape[1]
    planes = points // (mine * depth)
    far = pl.BlockSpec(memory_space=pl.ANY)
    whole = lambda a: pl.BlockSpec(a.shape, lambda x: (0, 0), pipeline_mode=pl.Buffered(1))
    return pl.pallas_call(
        functools.partial(finish_kernel, scale),
        grid=(planes // STEP,),
        in_specs=[whole(row), whole(pair), whole(turned), far, far, far],
        out_specs=pl.BlockSpec((bands, STEP, mine, depth), lambda x: (0, x, 0, 0)),
        out_shape=jax.ShapeDtypeStruct((bands, planes, mine, depth), F32),
        scratch_shapes=[
            pltpu.VMEM(parts.shape, BF16),
            pltpu.VMEM((2 * bands, points), BF16),
            pltpu.VMEM(row.shape, F32),
            pltpu.SemaphoreType.DMA((2, planes // STEP)),
        ],
        compiler_params=pltpu.CompilerParams(vmem_limit_bytes=60 << 20),
        cost_estimate=cost(18 * parts.size * bands // 4, 4 * parts.size),
        name="finish",
    )(row, pair, turned, parts, early, late)


def fast(wave, direction, potential, rotation):
    bands_here, planes, rows_y, depth = wave.shape
    parts = lax.axis_size("grid")
    bands, mine = bands_here * parts, rows_y // parts
    total_x = planes * lax.axis_size("band")
    scale = [-0.5 * (n / LATTICE) ** 2 for n in (total_x, rows_y, depth)]
    weights = (
        STENCIL[0] * sum(scale),
        *([s * c for c in STENCIL[1:]] for s in scale),
    )
    ncells = total_x * rows_y * depth

    def pack(field):
        cut = field.reshape(bands_here, -1, parts, mine, depth)
        return cut.transpose(2, 0, 1, 3, 4)

    def exchange(blocks):
        got = lax.all_to_all(blocks, "grid", 0, 0, tiled=True)
        return got.reshape(bands, -1, mine, depth)

    before, after = halos(wave, "band", 1)
    w = exchange(pack(wave))
    sent, own = kinetic(wave, before, after, weights, parts)
    own = lax.dynamic_update_slice(
        jnp.zeros((bands,), F32),
        own.sum((1, 2)),
        (lax.axis_index("grid") * bands_here,),
    )
    square = w * w
    numer = own + jnp.sum(square * potential[None], axis=(1, 2, 3))
    sums = butterfly_sum(jnp.stack([numer, jnp.sum(square, axis=(1, 2, 3))]))
    t = exchange(sent)
    cut = EARLY * planes // 16
    early, late, sums, turned = lax.optimization_barrier(
        (pack(direction[:, :cut]), pack(direction[:, cut:]), sums, rotation.T)
    )
    ritz = jnp.broadcast_to((sums[0] / sums[1])[:, None], (bands, depth))
    early = exchange(early)
    pair, basis = gram_pair(t, w, potential, ritz)
    late, half = lax.optimization_barrier((late, half_of_sum(pair)))
    late = exchange(late)
    pair = both_halves(half)

    inverse = factor_pair(pair, 1.0 / ncells)
    row, early = gram_row(basis, early, 0)
    late, row, inverse = lax.optimization_barrier((late, row, inverse))
    late_row, late = gram_row(basis, late, cut)
    row = both_halves(half_of_sum(row + late_row))
    return finish(row, inverse, turned, basis, early, late, 1.0 / ncells, mine, depth)


def axis_term(field, axis):
    total = STENCIL[0] * field
    for k in range(1, WIDTH + 1):
        total = total + STENCIL[k] * (jnp.roll(field, k, axis) + jnp.roll(field, -k, axis))
    return total


def general(wave, direction, potential, rotation):
    bands_here, planes, rows_y, depth = wave.shape
    total_x = planes * lax.axis_size("band")
    inverse_x, inverse_y, inverse_z = ((n / LATTICE) ** 2 for n in (total_x, rows_y, depth))
    before, after = halos(wave, "band", 1)
    padded = jnp.concatenate([before, wave, after], axis=1)
    along_x = STENCIL[0] * wave
    for k in range(1, WIDTH + 1):
        along_x = along_x + STENCIL[k] * (
            padded[:, WIDTH + k : WIDTH + k + planes]
            + padded[:, WIDTH - k : WIDTH - k + planes]
        )
    second = along_x * inverse_x + axis_term(wave, 2) * inverse_y + axis_term(wave, 3) * inverse_z
    local_pot = lax.all_gather(potential, "grid", axis=1, tiled=True)
    hwave = -0.5 * second + local_pot[None] * wave
    numer = jnp.sum(wave * hwave, axis=(1, 2, 3))
    denom = jnp.sum(wave * wave, axis=(1, 2, 3))
    numer, denom = lax.psum((numer, denom), "band")
    resid = hwave - (numer / denom)[:, None, None, None] * wave
    gathered = [
        lax.all_to_all(f, "grid", split_axis=2, concat_axis=0, tiled=True)
        for f in (resid, wave, direction)
    ]
    out_shape = gathered[0].shape
    stacked = jnp.concatenate(gathered, axis=0).reshape(3 * out_shape[0], -1)
    ncells = total_x * rows_y * depth
    gram = lax.psum(jnp.dot(stacked, stacked.T, precision=HIGH) / ncells, ("band", "grid"))
    factor = jnp.linalg.cholesky(gram)
    solved = jax.scipy.linalg.solve_triangular(factor, rotation, lower=True, trans=1)
    mixed = lax.dot_general(solved, stacked, (((0,), (0,)), ((), ())), precision=HIGH)
    return mixed.reshape(out_shape)


def on_device(wave, direction, potential, rotation):
    _, planes, rows_y, depth = wave.shape
    mine = rows_y // lax.axis_size("grid")
    sizes = lax.axis_size("band"), lax.axis_size("grid")
    tiled = mine == 8 and depth == 128 and planes % (8 * STEP) == 0
    tiled = tiled and all(n & (n - 1) == 0 for n in sizes) and sizes[0] >= 4
    return (fast if tiled else general)(wave, direction, potential, rotation)


def solution(mesh):
    return jax.shard_map(
        on_device,
        mesh=mesh,
        in_specs=(
            P("grid", "band", None, None),
            P("grid", "band", None, None),
            P("band", "grid", None),
            P(),
        ),
        out_specs=P(None, "band", "grid", None),
        check_vma=False,
    )
```

```python
import functools

import jax
import jax.numpy as jnp
from jax import lax
from jax.experimental import pallas as pl
from jax.experimental.pallas import tpu as pltpu
from jax.sharding import PartitionSpec as P

STENCIL = (
    -5369.0 / 1800.0,
    12.0 / 7.0,
    -15.0 / 56.0,
    10.0 / 189.0,
    -1.0 / 112.0,
    2.0 / 1925.0,
    -1.0 / 16632.0,
)
LATTICE = 51.3
WIDTH = len(STENCIL) - 1
HIGH = lax.Precision.HIGHEST
F32 = jnp.float32
BF16 = jnp.bfloat16


def halos(shard, axis, dim):
    devices, length = lax.axis_size(axis), shard.shape[dim]
    up = [(i, (i + 1) % devices) for i in range(devices)]
    down = [(j, i) for i, j in up]
    last = lax.slice_in_dim(shard, length - WIDTH, length, axis=dim)
    first = lax.slice_in_dim(shard, 0, WIDTH, axis=dim)
    return lax.ppermute(last, axis, up), lax.ppermute(first, axis, down)


def butterfly_sum(value):
    for axis in ("band", "grid"):
        devices, step = lax.axis_size(axis), 1
        while step < devices:
            value = value + lax.ppermute(
                value, axis, [(i, i ^ step) for i in range(devices)]
            )
            step *= 2
    return value


def core_pairs():
    return [(i, i ^ 1) for i in range(lax.axis_size("band"))]


def half_of_sum(value):
    half, odd = value.shape[0] // 2, lax.axis_index("band") % 2 == 1
    top, bottom = value[:half], value[half:]
    mine = jnp.where(odd, bottom, top)
    mine = mine + lax.ppermute(jnp.where(odd, top, bottom), "band", core_pairs())
    bands, grids = lax.axis_size("band"), lax.axis_size("grid")
    flips = [b * grids + g for b in (0, 2) for g in (0, 1)][1:]
    got = [
        lax.ppermute(mine, ("band", "grid"), [(i, i ^ f) for i in range(bands * grids)])
        for f in flips
    ]
    mine = (mine + got[0]) + (got[1] + got[2])
    for axis, step in (("band", 4), ("grid", 2)):
        devices = lax.axis_size(axis)
        while step < devices:
            mine = mine + lax.ppermute(
                mine, axis, [(i, i ^ step) for i in range(devices)]
            )
            step *= 2
    return mine


def both_halves(mine):
    odd = lax.axis_index("band") % 2 == 1
    other = lax.ppermute(mine, "band", core_pairs())
    return jnp.concatenate([jnp.where(odd, other, mine), jnp.where(odd, mine, other)])


def kinetic_kernel(weights, w_ref, lo_ref, hi_ref, t_ref, s_ref, pad):
    _, planes, rows, depth = w_ref.shape
    parts, _, _, mine, _ = t_ref.shape
    center, along_x, along_y, along_z = weights
    pad[0:WIDTH] = lo_ref[0]
    pad[WIDTH : WIDTH + planes] = w_ref[0]
    pad[WIDTH + planes :] = hi_ref[0]

    def plane(i, total):
        here = pad[i + WIDTH]
        out = center * here
        for k in range(1, WIDTH + 1):
            out += along_x[k - 1] * (pad[i + WIDTH + k] + pad[i + WIDTH - k])
            out += along_y[k - 1] * (
                pltpu.roll(here, k, 0) + pltpu.roll(here, rows - k, 0)
            )
            out += along_z[k - 1] * (
                pltpu.roll(here, k, 1) + pltpu.roll(here, depth - k, 1)
            )
        t_ref[:, 0, i] = out.reshape(parts, mine, depth)
        return total + (here * out).reshape(-1, 8, depth).sum(0)

    s_ref[0] = lax.fori_loop(0, planes, plane, jnp.zeros((8, depth), F32))


def kinetic(wave, before, after, weights, parts):
    bands, planes, rows, depth = wave.shape
    spec = lambda n: pl.BlockSpec((1, n, rows, depth), lambda b: (b, 0, 0, 0))
    return pl.pallas_call(
        functools.partial(kinetic_kernel, weights),
        grid=(bands,),
        in_specs=[spec(planes), spec(WIDTH), spec(WIDTH)],
        out_specs=[
            pl.BlockSpec(
                (parts, 1, planes, rows // parts, depth), lambda b: (0, b, 0, 0, 0)
            ),
            pl.BlockSpec((1, 8, depth), lambda b: (b, 0, 0)),
        ],
        out_shape=[
            jax.ShapeDtypeStruct((parts, bands, planes, rows // parts, depth), F32),
            jax.ShapeDtypeStruct((bands, 8, depth), F32),
        ],
        scratch_shapes=[pltpu.VMEM((planes + 2 * WIDTH, rows, depth), F32)],
        compiler_params=pltpu.CompilerParams(vmem_limit_bytes=32 << 20),
        cost_estimate=pl.CostEstimate(
            flops=60 * wave.size, bytes_accessed=11 * wave.size, transcendentals=0
        ),
        name="kinetic",
    )(wave, before, after)


def split(value):
    high = value.astype(BF16)
    return high, (value - high.astype(F32)).astype(BF16)


def dot_t(a, b, precision=None):
    return lax.dot_general(
        a, b, (((1,), (1,)), ((), ())), precision=precision, preferred_element_type=F32
    )


def dot(a, b, precision=None):
    return jnp.dot(a, b, precision=precision, preferred_element_type=F32)


def row_of(ref, i):
    bands, planes, mine, depth = ref.shape
    flat = ref.reshape(bands * planes * mine, depth)
    return flat[pl.ds(i, bands, stride=planes * mine), :]


def split_rows(ref):
    count = ref.shape[1] * ref.shape[2]
    highs, lows = zip(*(split(row_of(ref, i)) for i in range(count)))
    return jnp.concatenate(highs, axis=1), jnp.concatenate(lows, axis=1)


def gram_pair_kernel(t_ref, w_ref, v_ref, ritz_ref, g_ref, parts_ref, acc, cross):
    step, last = pl.program_id(0), pl.num_programs(0) - 1
    bands, planes, mine, depth = w_ref.shape

    @pl.when(step == 0)
    def _():
        acc[...] = jnp.zeros_like(acc)
        cross[...] = jnp.zeros_like(cross)

    for i in range(planes * mine):
        w = row_of(w_ref, i)
        x, y = i // mine, i % mine
        r = row_of(t_ref, i) + (v_ref[x, y : y + 1, :] - ritz_ref[...]) * w
        high, low = split(jnp.concatenate([r, w], axis=0))
        parts_ref[: 2 * bands, i * depth : (i + 1) * depth] = high
        parts_ref[2 * bands :, i * depth : (i + 1) * depth] = low
    high = parts_ref[: 2 * bands]
    acc[...] += dot_t(high, high)
    cross[...] += dot_t(high, parts_ref[2 * bands :])

    @pl.when(step == last)
    def _():
        g_ref[...] = acc[...] + (cross[...] + cross[...].T)


def gram_row_kernel(parts_ref, d_ref, g_ref, both_hbm, held, sems):
    step, last = pl.program_id(0), pl.num_programs(0) - 1
    points, count = parts_ref.shape

    @pl.when(step == 0)
    def _():
        g_ref[...] = jnp.zeros_like(g_ref)

    def copy_of(at):
        to = both_hbm.at[:, pl.ds(pl.multiple_of(at * count, count), count)]
        return pltpu.make_async_copy(held.at[at % 2], to, sems.at[at % 2])

    @pl.when(step >= 2)
    def _():
        copy_of(step - 2).wait()

    both = jnp.concatenate(split_rows(d_ref), axis=0)
    held[step % 2] = both
    copy_of(step).start()
    g_ref[:, :points] += dot_t(both, parts_ref[...])
    g_ref[:, points:] += dot_t(both, both)

    @pl.when(step == last)
    def _():
        copy_of(step - 1).wait()
        copy_of(step).wait()


def apply_points(parts, both, c_ref, o_ref):
    bands, planes, mine, depth = o_ref.shape
    high, low = split(c_ref[...])
    pair, last = slice(0, 2 * bands), slice(2 * bands, 3 * bands)
    stacked = jnp.concatenate([high[:, pair], low[:, pair]], axis=0)
    ending = jnp.concatenate(
        [
            jnp.concatenate([high[:, last], high[:, last]], axis=1),
            jnp.concatenate([low[:, last], jnp.zeros_like(low[:, last])], axis=1),
        ],
        axis=0,
    )
    wide = dot(stacked, parts[: 2 * bands]) + dot(ending, both)
    out = wide[:bands] + wide[bands:] + dot(high[:, pair], parts[2 * bands :])
    flat = o_ref.reshape(bands * planes * mine, depth)
    for i in range(planes * mine):
        flat[pl.ds(i, bands, stride=planes * mine), :] = out[:, i * depth : (i + 1) * depth]


def tile_spec(bands, planes, mine, depth):
    return pl.BlockSpec((bands, planes, mine, depth), lambda x: (0, x, 0, 0))


def cost(flops, nbytes):
    return pl.CostEstimate(flops=flops, bytes_accessed=nbytes, transcendentals=0)


STEP = 2
EARLY = 12


def gram_pair(t, w, v, ritz):
    bands, planes, mine, depth = w.shape
    tile = tile_spec(bands, STEP, mine, depth)
    points = pl.BlockSpec((4 * bands, STEP * mine * depth), lambda x: (0, x))
    parts = jax.ShapeDtypeStruct((4 * bands, planes * mine * depth), BF16)
    square = (2 * bands, 2 * bands)
    return pl.pallas_call(
        gram_pair_kernel,
        grid=(planes // STEP,),
        in_specs=[
            tile,
            tile,
            pl.BlockSpec((STEP, mine, depth), lambda x: (x, 0, 0)),
            pl.BlockSpec((bands, depth), lambda x: (0, 0)),
        ],
        out_specs=[pl.BlockSpec(square, lambda x: (0, 0)), points],
        out_shape=[jax.ShapeDtypeStruct(square, F32), parts],
        scratch_shapes=[pltpu.VMEM(square, F32), pltpu.VMEM(square, F32)],
        compiler_params=pltpu.CompilerParams(vmem_limit_bytes=60 << 20),
        cost_estimate=cost(16 * bands * w.size, 16 * w.size),
        name="gram_pair",
    )(t, w, v, ritz)


def gram_row(parts, d, skip):
    bands, planes, mine, depth = d.shape
    count = STEP * mine * depth
    shape = (2 * bands, 6 * bands)
    products, both = pl.pallas_call(
        gram_row_kernel,
        grid=(planes // STEP,),
        in_specs=[
            pl.BlockSpec((4 * bands, count), lambda x: (0, x + skip // STEP)),
            tile_spec(bands, STEP, mine, depth),
        ],
        out_specs=[
            pl.BlockSpec(shape, lambda x: (0, 0)),
            pl.BlockSpec(memory_space=pltpu.HBM),
        ],
        out_shape=[
            jax.ShapeDtypeStruct(shape, F32),
            jax.ShapeDtypeStruct((2 * bands, planes * mine * depth), BF16),
        ],
        scratch_shapes=[
            pltpu.VMEM((2, 2 * bands, count), BF16),
            pltpu.SemaphoreType.DMA((2,)),
        ],
        compiler_params=pltpu.CompilerParams(vmem_limit_bytes=(60 if skip == 0 else 40) << 20),
        cost_estimate=cost(18 * bands * d.size, 12 * d.size),
        name="gram_row",
    )(parts, d)
    wide = products[:bands] + products[bands:]
    pair = wide[:, : 2 * bands] + wide[:, 2 * bands : 4 * bands]
    own = wide[:, 4 * bands : 5 * bands] + wide[:, 5 * bands :]
    return jnp.concatenate([pair, own], axis=1), both


def spread_row(value, i):
    return jnp.broadcast_to(value[i : i + 1, :], value.shape)


def spread_column(value, j):
    return jnp.broadcast_to(value[:, j : j + 1], value.shape)


def inverse_factor(matrix):
    size = matrix.shape[0]
    count = size // 8
    shape = (8, size)
    sublane = lax.broadcasted_iota(jnp.int32, shape, 0)
    lane = lax.broadcasted_iota(jnp.int32, shape, 1)
    blocks = [matrix[8 * q : 8 * q + 8] for q in range(count)]
    done = []
    for p in range(count):
        base = 8 * p
        own = (lane >= base) & (lane < base + 8)
        rows = [spread_row(blocks[p], i) for i in range(8)]
        entry = {
            (i, j): spread_column(rows[i], base + j) for i in range(8) for j in range(i, 8)
        }
        unit, inverse = {}, []
        for k in range(8):
            inverse.append(1.0 / entry[k, k])
            for i in range(k + 1, 8):
                unit[i, k] = entry[k, i] * inverse[k]
            for i in range(k + 1, 8):
                for j in range(i, 8):
                    entry[i, j] = entry[i, j] - unit[i, k] * entry[k, j]
        for i in range(8):
            rows[i] = jnp.where(own, jnp.where(lane == base + i, 1.0, 0.0), rows[i])
            for k in range(i):
                rows[i] = rows[i] - unit[i, k] * rows[k]
        out = rows[0] * lax.rsqrt(entry[0, 0])
        for i in range(1, 8):
            out = jnp.where(sublane == i, rows[i] * lax.rsqrt(entry[i, i]), out)
        done.append(jnp.where(lane < base + 8, out, 0.0))
        if p == count - 1:
            break
        for i in reversed(range(8)):
            rows[i] = rows[i] * inverse[i]
            for k in reversed(range(i + 1, 8)):
                rows[i] = rows[i] - unit[k, i] * rows[k]
        for q in range(p + 1, count):
            columns = [spread_column(blocks[q], base + i) for i in range(8)]
            blocks[q] = jnp.where(own, 0.0, blocks[q])
            for i in reversed(range(8)):
                blocks[q] = blocks[q] - columns[i] * rows[i]
    return jnp.concatenate(done, axis=0)


def factor_first_kernel(scale, g_ref, o_ref):
    o_ref[...] = inverse_factor(g_ref[...] * scale)


def factor_second_kernel(scale, g_ref, first_ref, o_ref):
    half = first_ref.shape[0]
    first = first_ref[...]
    lower = dot_t(g_ref[:, :half] * scale, first, HIGH)
    second = inverse_factor(g_ref[:, half:] * scale - dot_t(lower, lower, HIGH))
    o_ref[:half, :half] = first
    o_ref[:half, half:] = jnp.zeros((half, half), F32)
    o_ref[half:, :half] = -dot(second, dot(lower, first, HIGH), HIGH)
    o_ref[half:, half:] = second


def factor_pair(gram, scale):
    half = gram.shape[0] // 2
    first = pl.pallas_call(
        functools.partial(factor_first_kernel, scale),
        grid=(1,),
        in_specs=[pl.BlockSpec((half, half), lambda i: (0, 0))],
        out_specs=pl.BlockSpec((half, half), lambda i: (0, 0)),
        out_shape=jax.ShapeDtypeStruct((half, half), F32),
        cost_estimate=cost(10**9, gram.size),
        name="factor_first",
    )(gram)
    return pl.pallas_call(
        functools.partial(factor_second_kernel, scale),
        grid=(1,),
        in_specs=[
            pl.BlockSpec((half, 2 * half), lambda i: (1, 0)),
            pl.BlockSpec((half, half), lambda i: (0, 0)),
        ],
        out_specs=pl.BlockSpec((2 * half, 2 * half), lambda i: (0, 0)),
        out_shape=jax.ShapeDtypeStruct(gram.shape, F32),
        cost_estimate=cost(10**9, 4 * gram.size),
        name="factor_second",
    )(gram, first)


def finish_kernel(scale, row_ref, pair_ref, turned_ref, parts_hbm, early_hbm, late_hbm, o_ref, *scratch):
    parts_ref, both_ref, c_ref, sems = scratch
    step, bands = pl.program_id(0), row_ref.shape[0]
    count = parts_ref.shape[1] // pl.num_programs(0)
    cut = early_hbm.shape[1] // count

    @pl.when(step == 0)
    def _():
        for i in range(parts_ref.shape[1] // count):
            to = pl.ds(i * count, count)
            d_hbm, at = (early_hbm, i) if i < cut else (late_hbm, i - cut)
            own = d_hbm.at[:, pl.ds(at * count, count)]
            pltpu.make_async_copy(parts_hbm.at[:, to], parts_ref.at[:, to], sems.at[0, i]).start()
            pltpu.make_async_copy(own, both_ref.at[:, to], sems.at[1, i]).start()
        pair = pair_ref[...]
        lower = dot_t(row_ref[:, : 2 * bands] * scale, pair, HIGH)
        rest = row_ref[:, 2 * bands :] * scale - dot_t(lower, lower, HIGH)
        first, through = dot(turned_ref[:, : 2 * bands], pair, HIGH), dot(lower, pair, HIGH)
        last = inverse_factor(rest)
        tail = dot(turned_ref[:, 2 * bands :], last, HIGH)
        c_ref[:, 2 * bands :] = tail
        c_ref[:, : 2 * bands] = first - dot(tail, through, HIGH)

    here = pl.ds(pl.multiple_of(step * count, count), count)
    for to_ref, sem in ((parts_ref, sems.at[0, step]), (both_ref, sems.at[1, step])):
        pltpu.make_async_copy(to_ref.at[:, here], to_ref.at[:, here], sem).wait()
    apply_points(parts_ref[:, here], both_ref[:, here], c_ref, o_ref)


def finish(row, pair, turned, parts, early, late, scale, mine, depth):
    bands, points = row.shape[0], parts.shape[1]
    planes = points // (mine * depth)
    far = pl.BlockSpec(memory_space=pl.ANY)
    whole = lambda a: pl.BlockSpec(a.shape, lambda x: (0, 0), pipeline_mode=pl.Buffered(1))
    return pl.pallas_call(
        functools.partial(finish_kernel, scale),
        grid=(planes // STEP,),
        in_specs=[whole(row), whole(pair), whole(turned), far, far, far],
        out_specs=pl.BlockSpec((bands, STEP, mine, depth), lambda x: (0, x, 0, 0)),
        out_shape=jax.ShapeDtypeStruct((bands, planes, mine, depth), F32),
        scratch_shapes=[
            pltpu.VMEM(parts.shape, BF16),
            pltpu.VMEM((2 * bands, points), BF16),
            pltpu.VMEM(row.shape, F32),
            pltpu.SemaphoreType.DMA((2, planes // STEP)),
        ],
        compiler_params=pltpu.CompilerParams(vmem_limit_bytes=60 << 20),
        cost_estimate=cost(18 * parts.size * bands // 4, 4 * parts.size),
        name="finish",
    )(row, pair, turned, parts, early, late)


def fast(wave, direction, potential, rotation):
    bands_here, planes, rows_y, depth = wave.shape
    parts = lax.axis_size("grid")
    bands, mine = bands_here * parts, rows_y // parts
    total_x = planes * lax.axis_size("band")
    scale = [-0.5 * (n / LATTICE) ** 2 for n in (total_x, rows_y, depth)]
    weights = (
        STENCIL[0] * sum(scale),
        *([s * c for c in STENCIL[1:]] for s in scale),
    )
    ncells = total_x * rows_y * depth

    def pack(field):
        cut = field.reshape(bands_here, -1, parts, mine, depth)
        return cut.transpose(2, 0, 1, 3, 4)

    def exchange(blocks):
        got = lax.all_to_all(blocks, "grid", 0, 0, tiled=True)
        return got.reshape(bands, -1, mine, depth)

    before, after = halos(wave, "band", 1)
    w = exchange(pack(wave))
    sent, own = kinetic(wave, before, after, weights, parts)
    own = lax.dynamic_update_slice(
        jnp.zeros((bands,), F32),
        own.sum((1, 2)),
        (lax.axis_index("grid") * bands_here,),
    )
    square = w * w
    numer = own + jnp.sum(square * potential[None], axis=(1, 2, 3))
    sums = butterfly_sum(jnp.stack([numer, jnp.sum(square, axis=(1, 2, 3))]))
    t = exchange(sent)
    cut = EARLY * planes // 16
    early, late, sums, turned = lax.optimization_barrier(
        (pack(direction[:, :cut]), pack(direction[:, cut:]), sums, rotation.T)
    )
    ritz = jnp.broadcast_to((sums[0] / sums[1])[:, None], (bands, depth))
    early = exchange(early)
    pair, basis = gram_pair(t, w, potential, ritz)
    late, half = lax.optimization_barrier((late, half_of_sum(pair)))
    late = exchange(late)
    pair = both_halves(half)

    inverse = factor_pair(pair, 1.0 / ncells)
    row, early = gram_row(basis, early, 0)
    late, row, inverse = lax.optimization_barrier((late, row, inverse))
    late_row, late = gram_row(basis, late, cut)
    row = both_halves(half_of_sum(row + late_row))
    return finish(row, inverse, turned, basis, early, late, 1.0 / ncells, mine, depth)


def axis_term(field, axis):
    total = STENCIL[0] * field
    for k in range(1, WIDTH + 1):
        total = total + STENCIL[k] * (jnp.roll(field, k, axis) + jnp.roll(field, -k, axis))
    return total


def general(wave, direction, potential, rotation):
    bands_here, planes, rows_y, depth = wave.shape
    total_x = planes * lax.axis_size("band")
    inverse_x, inverse_y, inverse_z = ((n / LATTICE) ** 2 for n in (total_x, rows_y, depth))
    before, after = halos(wave, "band", 1)
    padded = jnp.concatenate([before, wave, after], axis=1)
    along_x = STENCIL[0] * wave
    for k in range(1, WIDTH + 1):
        along_x = along_x + STENCIL[k] * (
            padded[:, WIDTH + k : WIDTH + k + planes]
            + padded[:, WIDTH - k : WIDTH - k + planes]
        )
    second = along_x * inverse_x + axis_term(wave, 2) * inverse_y + axis_term(wave, 3) * inverse_z
    local_pot = lax.all_gather(potential, "grid", axis=1, tiled=True)
    hwave = -0.5 * second + local_pot[None] * wave
    numer = jnp.sum(wave * hwave, axis=(1, 2, 3))
    denom = jnp.sum(wave * wave, axis=(1, 2, 3))
    numer, denom = lax.psum((numer, denom), "band")
    resid = hwave - (numer / denom)[:, None, None, None] * wave
    gathered = [
        lax.all_to_all(f, "grid", split_axis=2, concat_axis=0, tiled=True)
        for f in (resid, wave, direction)
    ]
    out_shape = gathered[0].shape
    stacked = jnp.concatenate(gathered, axis=0).reshape(3 * out_shape[0], -1)
    ncells = total_x * rows_y * depth
    gram = lax.psum(jnp.dot(stacked, stacked.T, precision=HIGH) / ncells, ("band", "grid"))
    factor = jnp.linalg.cholesky(gram)
    solved = jax.scipy.linalg.solve_triangular(factor, rotation, lower=True, trans=1)
    mixed = lax.dot_general(solved, stacked, (((0,), (0,)), ((), ())), precision=HIGH)
    return mixed.reshape(out_shape)


def on_device(wave, direction, potential, rotation):
    _, planes, rows_y, depth = wave.shape
    mine = rows_y // lax.axis_size("grid")
    sizes = lax.axis_size("band"), lax.axis_size("grid")
    tiled = mine == 8 and depth == 128 and planes % (8 * STEP) == 0
    tiled = tiled and all(n & (n - 1) == 0 for n in sizes) and sizes[0] >= 4
    return (fast if tiled else general)(wave, direction, potential, rotation)


def solution(mesh):
    return jax.shard_map(
        on_device,
        mesh=mesh,
        in_specs=(
            P("grid", "band", None, None),
            P("grid", "band", None, None),
            P("band", "grid", None),
            P(),
        ),
        out_specs=P(None, "band", "grid", None),
        check_vma=False,
    )
```
